32 devices in a mesh: seq: 16 (over z, y, x), mp: 2 (over core).
Axes of the slice: x: 2, y: 2, z: 4, core: 2. Of those that a mesh axis runs over, the one named last changes fastest.
Arguments:
- bytes_in: bfloat16 [16384, 1024], P('seq'), may hold values from -6 to 6
- out_grad: bfloat16 [16384, 1024], P('seq'), may hold values from -6 to 6
- seq_ids: int32 [2048], replicated, may hold values from 0 to 5, never falling along the last dimension, each value on 1 to 1024 neighbouring positions
- norm_gain: float32 [1024], P('seq'), may hold values from 0.5 to 1.5
- w_z: float32 [1024, 2048], P('seq', 'mp'), may hold values from -0.1875 to 0.1875
- w_x: float32 [1024, 2048], P('seq', 'mp'), may hold values from -0.1875 to 0.1875
- w_bc: float32 [1024, 256], P('seq'), may hold values from -0.1875 to 0.1875
- w_dt: float32 [1024, 32], P('seq', 'mp'), may hold values from -0.1875 to 0.1875
- w_out: float32 [2048, 1024], P('mp', 'seq'), may hold values from -0.125 to 0.125
- attn_gain: float32 [1024], P('seq'), may hold values from 0.5 to 1.5
- w_q: float32 [1024, 1024], P('seq', 'mp'), may hold values from -0.1875 to 0.1875
- w_k: float32 [1024, 1024], P('seq', 'mp'), may hold values from -0.1875 to 0.1875
- w_v: float32 [1024, 1024], P('seq', 'mp'), may hold values from -0.1875 to 0.1875
- w_o: float32 [1024, 1024], P('mp', 'seq'), may hold values from -0.5 to 0.5
- mlp_gain: float32 [1024], P('seq'), may hold values from 0.5 to 1.5
- w_gate: float32 [1024, 4096], P('seq', 'mp'), may hold values from -0.1875 to 0.1875
- w_up: float32 [1024, 4096], P('seq', 'mp'), may hold values from -0.1875 to 0.1875
- w_down: float32 [4096, 1024], P('mp', 'seq'), may hold values from -0.09375 to 0.09375
- dt_bias: float32 [32], P('mp'), may hold values from -1 to 1
- a_log: float32 [32], P('mp')
- d_skip: float32 [32], P('mp'), may hold values from 0.5 to 1.5
- conv_x: float32 [4, 2048], P(None, 'mp'), may hold values from -3 to 3
- conv_bc: float32 [4, 256], replicated, may hold values from -3 to 3
- inner_gain: float32 [2048], P('mp'), may hold values from 0.5 to 1.5
Outputs:
- block_out: float32 [16384, 1024], P('seq')
- bytes_grad: float32 [16384, 1024], P('seq')
- norm_gain_grad: float32 [1024], P('seq')
- w_z_grad: float32 [1024, 2048], P('seq', 'mp')
- w_x_grad: float32 [1024, 2048], P('seq', 'mp')
- w_bc_grad: float32 [1024, 256], P('seq')
- w_dt_grad: float32 [1024, 32], P('seq', 'mp')
- w_out_grad: float32 [2048, 1024], P('mp', 'seq')
- attn_gain_grad: float32 [1024], P('seq')
- w_q_grad: float32 [1024, 1024], P('seq', 'mp')
- w_k_grad: float32 [1024, 1024], P('seq', 'mp')
- w_v_grad: float32 [1024, 1024], P('seq', 'mp')
- w_o_grad: float32 [1024, 1024], P('mp', 'seq')
- mlp_gain_grad: float32 [1024], P('seq')
- w_gate_grad: float32 [1024, 4096], P('seq', 'mp')
- w_up_grad: float32 [1024, 4096], P('seq', 'mp')
- w_down_grad: float32 [4096, 1024], P('mp', 'seq')
- dt_bias_grad: float32 [32], P('mp')
- a_log_grad: float32 [32], P('mp')
- d_skip_grad: float32 [32], P('mp')
- conv_x_grad: float32 [4, 2048], P(None, 'mp')
- conv_bc_grad: float32 [4, 256], replicated
- inner_gain_grad: float32 [2048], P('mp')
The draws below stay inside these ranges and needn't reach their ends.
Inputs may be any that keep to these rules, and one draw needn't show every extreme that they name: `seq_ids`: patches of one sequence are contiguous and ids never fall; every id appears; one sequence has exactly 1024 patches.
All inputs are finite; a program needn't handle non-finite values.
Results may differ from the reference program's by a relative error of at most 0.022.
Values may be sent and summed in bfloat16 or wider, within the bound.
No kernel may reach another device: no remote copies, remote signals or barrier semaphores. Data moves between devices by JAX's collectives and lax.ppermute only.
A program may use at most 256 MiB of HBM per device.

```python
import math
import jax
import jax.numpy as jnp
import numpy as np
from jax import lax

D = 1024
H = 32
NS = 128
KC = 4
LH = 16
LHD = 64
FF = 4096
PATCH = 8
NSEQ = 6
DI = 2048
BYTES = 16384
PATCHES = 2048
LONGEST = 1024


def draw_a_log(key, part):
    key_one, key_two, key_three = jax.random.split(key, 3)
    slow_share = 0.5
    slow_heads = jax.random.uniform(key_one, (H,)) < slow_share
    fast_rate = jax.random.uniform(key_two, (H,), minval=1.0 / 40.0, maxval=1.0 / 12.0)
    slow_rate = jax.random.uniform(key_three, (H,), minval=0.2, maxval=1.0) / LONGEST
    return jnp.log(jnp.where(slow_heads, slow_rate, fast_rate)).astype(jnp.float32)


def level_of(rng, extent, shards, low, largest):
    def one(position, parts):
        heights = jax.random.uniform(jax.random.fold_in(jax.random.fold_in(rng, 6), position), (parts,), jnp.float32, low / len(shards), largest / len(shards))
        return jnp.repeat(jnp.exp(heights), extent[position] // parts).reshape((-1,) + (1,) * (len(extent) - position - 1))

    loudness = one(*shards[0])
    for cut in shards[1:]:
        loudness = loudness * one(*cut)
    return loudness


def length_profile(amount, total, limit, slope):
    portions = [(1 << 20) // math.isqrt(grade ** slope) + 1 for grade in range(2, amount + 1)]
    rest, given = total - limit - (amount - 1), [1] * (amount - 1)
    while rest > 0:
        free = [i for i in range(amount - 1) if given[i] < limit]
        whole, remaining = sum([portions[i] for i in free]), rest
        for i in free:
            more = min(limit - given[i], max(1, remaining * portions[i] // whole), rest)
            given[i] = given[i] + more
            rest = rest - more
    return np.array([limit] + given)


def ragged_sizes(stream_key, number_of, total, limit, skew):
    if number_of == 2:
        one = jax.random.randint(stream_key, (), max(1, total - limit), min(limit, total - 1) + 1)
        return jnp.stack([one, total - one])
    tallies = jnp.asarray(length_profile(number_of, total, limit, skew), jnp.int32)
    pairs = (number_of - 1) // 2
    donor, receiver = tallies[1:1 + 2 * pairs:2], tallies[2:2 + 2 * pairs:2]
    margin = jnp.minimum(donor - 1, limit - receiver)
    moved = jax.random.randint(jax.random.fold_in(stream_key, 1), (pairs,), 0, 1 << 20) % (margin + 1)
    tallies = tallies.at[1:1 + 2 * pairs:2].set(donor - moved).at[2:2 + 2 * pairs:2].set(receiver + moved)
    return tallies[jax.random.permutation(jax.random.fold_in(stream_key, 2), number_of)]


def gaussian(stream_key, shape, width, most, cuts=(), dtype=jnp.bfloat16):
    result = jax.random.normal(stream_key, shape, jnp.float32) * width
    if len(cuts) > 0:
        result = level_of(stream_key, shape, cuts, -0.22, 0.18) * result
    return jnp.clip(result, min=-most, max=most).astype(dtype)


def setup_inputs(seed: int = 0) -> dict:
    streams_of = jax.random.split(jax.random.key(seed), 25)
    return {
        "bytes_in": gaussian(streams_of[0], (BYTES, D), 1.0, 6.0, ((0, 16),)),
        "out_grad": gaussian(streams_of[1], (BYTES, D), 1.0, 6.0, ((0, 16),)),
        "seq_ids": jnp.searchsorted(jnp.cumsum(ragged_sizes(streams_of[2], NSEQ, PATCHES, LONGEST, 2)), jnp.arange(PATCHES), side="right").astype(jnp.int32),
        "norm_gain": jnp.clip(1.0 + 0.1 * jax.random.normal(streams_of[3], (D,), jnp.float32), 0.5, 1.5),
        "w_z": gaussian(streams_of[4], (D, DI), D ** -0.5, 0.1875, ((0, 16), (1, 2)), jnp.float32),
        "w_x": gaussian(streams_of[5], (D, DI), D ** -0.5, 0.1875, ((0, 16), (1, 2)), jnp.float32),
        "w_bc": gaussian(streams_of[6], (D, 2 * NS), D ** -0.5, 0.1875, ((0, 16),), jnp.float32),
        "w_dt": gaussian(streams_of[7], (D, H), D ** -0.5, 0.1875, ((0, 16), (1, 2)), jnp.float32),
        "w_out": gaussian(streams_of[8], (DI, D), DI ** -0.5, 0.125, ((0, 2), (1, 16)), jnp.float32),
        "attn_gain": jnp.clip(1.0 + 0.1 * jax.random.normal(streams_of[9], (D,), jnp.float32), 0.5, 1.5),
        "w_q": gaussian(streams_of[10], (D, LH * LHD), D ** -0.5, 0.1875, ((0, 16), (1, 2)), jnp.float32),
        "w_k": gaussian(streams_of[11], (D, LH * LHD), D ** -0.5, 0.1875, ((0, 16), (1, 2)), jnp.float32),
        "w_v": gaussian(streams_of[12], (D, LH * LHD), D ** -0.5, 0.1875, ((0, 16), (1, 2)), jnp.float32),
        "w_o": gaussian(streams_of[13], (LH * LHD, D), (LH * LHD // PATCH) ** -0.5, 0.5, ((0, 2), (1, 16)), jnp.float32),
        "mlp_gain": jnp.clip(1.0 + 0.1 * jax.random.normal(streams_of[14], (D,), jnp.float32), 0.5, 1.5),
        "w_gate": gaussian(streams_of[15], (D, FF), D ** -0.5, 0.1875, ((0, 16), (1, 2)), jnp.float32),
        "w_up": gaussian(streams_of[16], (D, FF), D ** -0.5, 0.1875, ((0, 16), (1, 2)), jnp.float32),
        "w_down": gaussian(streams_of[17], (FF, D), FF ** -0.5, 0.09375, ((0, 2), (1, 16)), jnp.float32),
        "dt_bias": jnp.clip(jax.random.uniform(streams_of[18], (H,), jnp.float32, -1.0, 1.0) * level_of(streams_of[18], (H,), ((0, 2),), -0.4, 0.0), -1.0, 1.0),
        "a_log": draw_a_log(jax.random.fold_in(streams_of[24], 71), 0),
        "d_skip": jnp.clip(0.5 + 1.0 * jax.random.uniform(streams_of[20], (H,), jnp.float32) ** level_of(streams_of[20], (H,), ((0, 2),), -0.2, 0.2), 0.5, 1.5),
        "conv_x": gaussian(streams_of[21], (KC, DI), KC ** -0.5, 3.0, ((1, 2),), jnp.float32),
        "conv_bc": gaussian(streams_of[22], (KC, 2 * NS), KC ** -0.5, 3.0, (), jnp.float32),
        "inner_gain": jnp.clip(1.0 + 0.1 * jax.random.normal(streams_of[23], (DI,), jnp.float32), 0.5, 1.5),
    }


EPS = 1e-05
BIG = 1e+30
PRECISE = lax.Precision.HIGHEST

@jax.custom_vjp
def low(v):
    return lax.optimization_barrier(v.astype(jnp.bfloat16)).astype(jnp.float32)

@jax.custom_vjp
def low_back(v):
    return v

def low_keep(v):
    return (low(v), None)

def low_pass(kept, grad):
    return (grad,)

def back_keep(v):
    return (v, None)

def back_low(kept, grad):
    return (low(grad),)
low.defvjp(low_keep, low_pass)
low_back.defvjp(back_keep, back_low)

def matmul(left, right):
    return jnp.dot(left, right, precision=PRECISE, preferred_element_type=jnp.float32)

def rms_scale(values):
    return lax.rsqrt(lax.optimization_barrier(jnp.mean(values * values, axis=-1, keepdims=True)) + EPS)

def softplus_fn(values):
    return jnp.log1p(jnp.exp(-jnp.abs(values))) + jnp.maximum(values, 0.0)

def conv_taps(extended, ids_ext, kernel):
    conv_width = kernel.shape[0]
    row_count = extended.shape[0] - conv_width + 1
    target = ids_ext[conv_width - 1:]
    summed = jnp.zeros((row_count, extended.shape[1]), jnp.float32)
    for tap_index in range(conv_width):
        same_seg = (ids_ext[tap_index:tap_index + row_count] == target).astype(jnp.float32)
        summed = summed + extended[tap_index:tap_index + row_count] * kernel[tap_index][None, :] * same_seg[:, None]
    return summed

def ssd_block(x_heads, b_rows, c_rows, step_size, log_decay, seg_rows, prev_seg, d_skip):
    length = x_heads.shape[0]
    cum_decay = jnp.cumsum(log_decay, axis=0)
    cum_heads = cum_decay.T
    same_seg = seg_rows[:, None] == seg_rows[None, :]
    row_pos = lax.broadcasted_iota(jnp.int32, (length, length), 0)
    col_pos = lax.broadcasted_iota(jnp.int32, (length, length), 1)
    live_mask = same_seg & (row_pos >= col_pos)
    decay_gaps = cum_heads[:, :, None] - cum_heads[:, None, :]
    decay_mat = jnp.exp(jnp.where(live_mask[None], decay_gaps, -BIG))
    inner_prod = matmul(c_rows, b_rows.T)
    mix_mat = inner_prod[None] * decay_mat * step_size.T[:, None, :]
    y_local = jnp.einsum('hts,shp->thp', mix_mat, x_heads, precision=PRECISE) + d_skip[None, :, None] * x_heads
    carried = (seg_rows == prev_seg).astype(jnp.float32)
    decay_in = carried[:, None] * jnp.exp(cum_decay)
    end_same = seg_rows == seg_rows[length - 1]
    end_gap = cum_decay[length - 1][None, :] - cum_decay
    tail_w = jnp.exp(jnp.where(end_same[:, None], end_gap, -BIG)) * step_size
    state_local = jnp.einsum('shp,sn->hpn', x_heads * tail_w[:, :, None], b_rows, precision=PRECISE)
    return (y_local, decay_in, state_local, decay_in[length - 1])

def mamba_part(h_norm, seq_ids, w_z, w_x, w_bc, w_dt, w_out, dt_bias, a_log, d_skip, conv_x, conv_bc, inner_gain):
    row_count = h_norm.shape[0]
    gate_z = low_back(matmul(h_norm, low(w_z)))
    mixed_in = low_back(low(jnp.concatenate([matmul(h_norm, low(w_x)), matmul(h_norm, low(w_bc))], axis=1)))
    dt_raw = low_back(matmul(h_norm, low(w_dt)))
    conv_width = conv_x.shape[0]
    extended = jnp.concatenate([jnp.zeros((conv_width - 1, mixed_in.shape[1]), jnp.float32), mixed_in], axis=0)
    ids_ext = jnp.concatenate([jnp.full((conv_width - 1,), -1, jnp.int32), seq_ids])
    kernel = jnp.concatenate([conv_x, conv_bc], axis=1)
    activated = jax.nn.silu(conv_taps(extended, ids_ext, kernel))
    inner_width = conv_x.shape[1]
    head_count = a_log.shape[0]
    head_size = inner_width // head_count
    x_heads = activated[:, :inner_width].reshape(row_count, head_count, head_size)
    b_rows = activated[:, inner_width:inner_width + NS]
    c_rows = activated[:, inner_width + NS:]
    step_size = softplus_fn(dt_raw + dt_bias[None, :])
    log_decay = -step_size * jnp.exp(a_log)[None, :]
    block_rows = math.gcd(row_count, 128)
    block_count = row_count // block_rows
    pieces = (x_heads.reshape(block_count, block_rows, head_count, head_size), b_rows.reshape(block_count, block_rows, NS), c_rows.reshape(block_count, block_rows, NS), step_size.reshape(block_count, block_rows, head_count), log_decay.reshape(block_count, block_rows, head_count), seq_ids.reshape(block_count, block_rows))

    def run_block(carry_in, block_parts):
        state_now, prev_seg = carry_in
        x_block, b_block, c_block, step_block, decay_block, seg_block = block_parts
        y_local, decay_in, state_local, total_decay = ssd_block(x_block, b_block, c_block, step_block, decay_block, seg_block, prev_seg, d_skip)
        y_block = y_local + decay_in[:, :, None] * jnp.einsum('tn,hpn->thp', c_block, state_now, precision=PRECISE)
        new_state = total_decay[:, None, None] * state_now + state_local
        return ((new_state, seg_block[block_rows - 1]), y_block)
    start_carry = (jnp.zeros((head_count, head_size, NS), jnp.float32), jnp.int32(-1))
    final_carry, y_blocks = lax.scan(jax.checkpoint(run_block), start_carry, pieces)
    mixer_y = y_blocks.reshape(row_count, inner_width)
    gated_out = mixer_y * jax.nn.silu(gate_z)
    y_norm = low(gated_out * rms_scale(gated_out) * inner_gain[None, :])
    return low_back(matmul(y_norm, low(w_out)))

def local_part(rows_in, lowered):
    attn_gain, w_q, w_k, w_v, w_o, mlp_gain, w_gate, w_up, w_down = lowered
    row_count = rows_in.shape[0]
    shape_four = (row_count // PATCH, PATCH, LH, LHD)
    normed = low(rows_in * rms_scale(rows_in) * attn_gain[None, :])
    queries = low(low_back(matmul(normed, w_q))).reshape(shape_four)
    key_rows = low(low_back(matmul(normed, w_k))).reshape(shape_four)
    value_rows = low(low_back(matmul(normed, w_v))).reshape(shape_four)
    scores = low_back(jnp.einsum('bqhd,bkhd->bhqk', queries, key_rows, precision=PRECISE) * LHD ** (-0.5))
    row_pos = lax.broadcasted_iota(jnp.int32, (PATCH, PATCH), 0)
    col_pos = lax.broadcasted_iota(jnp.int32, (PATCH, PATCH), 1)
    masked = jnp.where((row_pos >= col_pos)[None, None], scores, -BIG)
    row_max = lax.optimization_barrier(jnp.max(masked, axis=-1, keepdims=True))
    exp_scores = jnp.exp(masked - row_max)
    soft_weights = exp_scores / lax.optimization_barrier(jnp.sum(exp_scores, axis=-1, keepdims=True))
    attended = low(low_back(jnp.einsum('bhqk,bkhd->bqhd', low(soft_weights), value_rows, precision=PRECISE)))
    attended = attended.reshape(row_count, LH * LHD)
    after_attn = rows_in + low_back(matmul(attended, w_o))
    normed_mlp = low(after_attn * rms_scale(after_attn) * mlp_gain[None, :])
    gate_val = low_back(matmul(normed_mlp, w_gate))
    up_val = low_back(matmul(normed_mlp, w_up))
    hidden = low(jax.nn.silu(gate_val) * up_val)
    return after_attn + low_back(matmul(hidden, w_down))

def forward(x_float, seq_ids, norm_gain, w_z, w_x, w_bc, w_dt, w_out, attn_gain, w_q, w_k, w_v, w_o, mlp_gain, w_gate, w_up, w_down, dt_bias, a_log, d_skip, conv_x, conv_bc, inner_gain):
    patch_in = lax.optimization_barrier(jnp.mean(x_float.reshape(PATCHES, PATCH, D), axis=1))
    h_norm = low(patch_in * rms_scale(patch_in) * low(norm_gain)[None, :])
    mixer_out = mamba_part(h_norm, seq_ids, w_z, w_x, w_bc, w_dt, w_out, dt_bias, a_log, d_skip, conv_x, conv_bc, inner_gain)
    patch_out = patch_in + mixer_out
    rows_in = x_float + jnp.repeat(patch_out, PATCH, axis=0)
    lowered = (low(attn_gain), low(w_q), low(w_k), low(w_v), low(w_o), low(mlp_gain), low(w_gate), low(w_up), low(w_down))
    block_rows = math.gcd(BYTES, 4096)

    def run_rows(rows_block):
        return local_part(rows_block, lowered)
    outputs = lax.map(jax.checkpoint(run_rows), rows_in.reshape(BYTES // block_rows, block_rows, D))
    return outputs.reshape(BYTES, D)

def reference(bytes_in, out_grad, seq_ids, norm_gain, w_z, w_x, w_bc, w_dt, w_out, attn_gain, w_q, w_k, w_v, w_o, mlp_gain, w_gate, w_up, w_down, dt_bias, a_log, d_skip, conv_x, conv_bc, inner_gain):
    x_float = bytes_in.astype(jnp.float32)

    def closed(x_part, *params):
        return forward(x_part, seq_ids, *params)
    block_out, pullback = jax.vjp(closed, x_float, norm_gain, w_z, w_x, w_bc, w_dt, w_out, attn_gain, w_q, w_k, w_v, w_o, mlp_gain, w_gate, w_up, w_down, dt_bias, a_log, d_skip, conv_x, conv_bc, inner_gain)
    grad_parts = pullback(out_grad.astype(jnp.float32))
    return (block_out, grad_parts[0], grad_parts[1], grad_parts[2], grad_parts[3], grad_parts[4], grad_parts[5], grad_parts[6], grad_parts[7], grad_parts[8], grad_parts[9], grad_parts[10], grad_parts[11], grad_parts[12], grad_parts[13], grad_parts[14], grad_parts[15], grad_parts[16], grad_parts[17], grad_parts[18], grad_parts[19], grad_parts[20], grad_parts[21])
```

```python
import functools

import jax
import jax.numpy as jnp
from jax import lax
from jax.sharding import PartitionSpec as P

LHD = 64
PATCH = 8
EPS = 1e-05
BIG = 1e30
PRECISE = lax.Precision.HIGHEST
BF = jnp.bfloat16
F32 = jnp.float32


def factors(count):
    root = 1
    while (root * 2) ** 3 <= count:
        root *= 2
    rest = count // root
    middle = root if rest % root == 0 and rest // root >= root else 1
    return (rest // middle, middle, root)


class Grid:
    def __init__(self, count):
        self.count = count
        self.sizes = factors(count)
        self.place = lax.axis_index("seq")
        n0, n1, n2 = self.sizes
        self.coord = (self.place // (n1 * n2), (self.place // n2) % n1, self.place % n2)

    def pairs(self, dim, by):
        n0, n1, n2 = self.sizes
        out = []
        for i in range(self.count):
            c = [i // (n1 * n2), (i // n2) % n1, i % n2]
            c[dim] = (c[dim] + by) % self.sizes[dim]
            out.append((i, (c[0] * n1 + c[1]) * n2 + c[2]))
        return out

    def shift(self, value, dim, by=1):
        return lax.ppermute(value, "seq", self.pairs(dim, by))


def spread(grid, block, dim):
    n = grid.sizes[dim]
    if n == 1:
        return block[None]
    got = [block]
    for _ in range(1, n):
        got.append(grid.shift(got[-1], dim))
    ring = jnp.stack(got[::-1] + got[:0:-1])
    return lax.dynamic_slice_in_dim(ring, n - 1 - grid.coord[dim], n, 0)


def gather_rows(grid, block, route, after=None):
    rows, width = block.shape
    if after is not None:
        block = lax.optimization_barrier((block, after))[0]
    mark = None
    for step, dim in enumerate(route):
        block = spread(grid, block, dim)
        if step == 1:
            mark = block
    order = list(reversed(route))
    block = jnp.transpose(block, [order.index(d) for d in range(3)] + [3, 4])
    return block.reshape(grid.count * rows, width), mark


def fold(grid, total, axis, dim):
    n = grid.sizes[dim]
    me = grid.coord[dim]

    def pick(k):
        return lax.dynamic_index_in_dim(total, (me + k) % n, axis, False)

    if n == 1:
        return pick(0)
    moving = pick(-1)
    for t in range(1, n):
        moving = grid.shift(moving, dim)
        moving = (moving.astype(F32) + pick(-1 - t).astype(F32)).astype(BF)
    return moving


def scatter_rows(grid, partial, route):
    n = partial.shape[1]
    rows = partial.shape[0] // grid.count
    left = [0, 1, 2]
    total = partial.astype(BF).reshape(grid.sizes + (rows, n))
    for dim in route:
        axis = left.index(dim)
        total = fold(grid, total, axis, dim)
        left.remove(dim)
    return total.astype(F32)


def swap_mp(value):
    size = lax.axis_size("mp")
    return lax.ppermute(value, "mp", [(i, (i + 1) % size) for i in range(size)])


def mp_sum(value):
    low = value.astype(BF)
    return low.astype(F32) + swap_mp(low).astype(F32)


def mp_sum_exact(value):
    return value + swap_mp(value)


def seq_sum(value):
    count = lax.axis_size("seq")
    by = 1
    while by < count:
        value = value + lax.ppermute(value, "seq", [(i, i ^ by) for i in range(count)])
        by *= 2
    return value


def combine(earlier, later):
    return (earlier[0] * later[0], later[0][:, None, None] * earlier[1] + later[1])


def pick_pair(flag, a, b):
    return jax.tree.map(lambda x, y: jnp.where(flag, x, y), a, b)


def scan_states(grid, decay, state, reverse):
    heads = decay.shape[0]
    shape = state.shape
    one = (jnp.ones_like(decay), jnp.zeros_like(state))

    def pack(pair):
        flat = pair[1].reshape(heads * shape[1], shape[2])
        tail = jnp.broadcast_to(pair[0][:, None], (heads, shape[2]))
        return jnp.concatenate([flat, tail], axis=0).astype(BF)

    def unpack(low):
        wide = low.astype(F32)
        return (wide[heads * shape[1] :, 0], wide[: heads * shape[1]].reshape(shape))

    total = (decay, state)
    enter = one
    dims = [d for d in (2, 1, 0) if grid.sizes[d] > 1]
    for dim in dims:
        n = grid.sizes[dim]
        me = grid.coord[dim]
        me = (n - 1 - me) if reverse else me
        moving = pack(total)
        before, after = one, one
        got = []
        for k in range(1, n):
            moving = grid.shift(moving, dim, -1 if reverse else 1)
            got.append(unpack(moving))
            enter_new = combine(got[-1], enter)
            enter = pick_pair(me >= k, enter_new, enter)
        if dim == dims[-1]:
            break
        own = unpack(pack(total))
        before = one
        for k in range(1, n):
            before = combine(pick_pair(me >= k, got[k - 1], one), before)
        after = one
        for k in range(n - 1, 0, -1):
            after = combine(after, pick_pair(me < k, got[k - 1], one))
        total = combine(before, combine(own, after))
    return enter


def bf_dot(left, right):
    return jnp.dot(left, right, preferred_element_type=F32)


def dot_t(left, right):
    return lax.dot_general(left, right, (((1,), (1,)), ((), ())), preferred_element_type=F32)


def grad_dot(left, right):
    return lax.dot_general(left, right, (((0,), (0,)), ((), ())), preferred_element_type=F32)


def rms_rows(values):
    return lax.rsqrt(jnp.mean(values * values, axis=-1, keepdims=True) + EPS)


def norm_back(grad_in, values, rstd_rows, gain_row):
    normed_rows = values * rstd_rows
    gain_grad = jnp.sum(grad_in * normed_rows, axis=0)
    scaled = grad_in * gain_row[None, :]
    input_grad = rstd_rows * (
        scaled - normed_rows * jnp.mean(scaled * normed_rows, axis=-1, keepdims=True)
    )
    return (input_grad, gain_grad)


def softplus_fn(values):
    return jnp.log1p(jnp.exp(-jnp.abs(values))) + jnp.maximum(values, 0.0)


def conv_taps(extended, ids_ext, kernel):
    conv_width = kernel.shape[0]
    row_count = extended.shape[0] - conv_width + 1
    target = ids_ext[conv_width - 1 :]
    summed = jnp.zeros((row_count, extended.shape[1]), F32)
    for tap_index in range(conv_width):
        same_seg = (ids_ext[tap_index : tap_index + row_count] == target).astype(F32)
        summed = (
            summed
            + extended[tap_index : tap_index + row_count]
            * kernel[tap_index][None, :]
            * same_seg[:, None]
        )
    return summed


def running_sum(values):
    length = values.shape[0]
    row = lax.broadcasted_iota(jnp.int32, (length, length), 0)
    col = lax.broadcasted_iota(jnp.int32, (length, length), 1)
    lower = (row >= col).astype(F32)
    return jnp.dot(lower, values, precision=PRECISE, preferred_element_type=F32)


def ssd_block(x_heads, b_rows, c_rows, step_size, log_decay, seg_rows, prev_seg, d_skip):
    length = x_heads.shape[0]
    cum_decay = running_sum(log_decay)
    cum_heads = cum_decay.T
    same_seg = seg_rows[:, None] == seg_rows[None, :]
    row_pos = lax.broadcasted_iota(jnp.int32, (length, length), 0)
    col_pos = lax.broadcasted_iota(jnp.int32, (length, length), 1)
    live_mask = same_seg & (row_pos >= col_pos)
    decay_gaps = cum_heads[:, :, None] - cum_heads[:, None, :]
    decay_mat = jnp.exp(jnp.where(live_mask[None], decay_gaps, -BIG))
    inner_prod = jnp.dot(c_rows, b_rows.T, precision=PRECISE, preferred_element_type=F32)
    mix_mat = inner_prod[None] * decay_mat * step_size.T[:, None, :]
    y_local = (
        jnp.einsum("hts,shp->thp", mix_mat, x_heads, precision=PRECISE)
        + d_skip[None, :, None] * x_heads
    )
    carried = (seg_rows == prev_seg).astype(F32)
    decay_in = carried[:, None] * jnp.exp(cum_decay)
    end_same = seg_rows == seg_rows[length - 1]
    end_gap = cum_decay[length - 1][None, :] - cum_decay
    tail_w = jnp.exp(jnp.where(end_same[:, None], end_gap, -BIG)) * step_size
    state_local = jnp.einsum("shp,sn->hpn", x_heads * tail_w[:, :, None], b_rows, precision=PRECISE)
    return (y_local, decay_in, state_local, decay_in[length - 1])


def soft_scores(queries, key_rows, shape_four):
    scale = LHD ** (-0.5)
    scores = (
        jnp.einsum(
            "bqhd,bkhd->bhqk",
            queries.reshape(shape_four),
            key_rows.reshape(shape_four),
            preferred_element_type=F32,
        )
        * scale
    )
    row_pos = lax.broadcasted_iota(jnp.int32, (PATCH, PATCH), 0)
    col_pos = lax.broadcasted_iota(jnp.int32, (PATCH, PATCH), 1)
    masked = jnp.where((row_pos >= col_pos)[None, None], scores, -BIG)
    row_max = jnp.max(masked, axis=-1, keepdims=True)
    exp_scores = jnp.exp(masked - row_max)
    return exp_scores / jnp.sum(exp_scores, axis=-1, keepdims=True)


def local(
    seq_count,
    bytes_in,
    out_grad,
    seq_ids,
    norm_gain,
    w_z,
    w_x,
    w_bc,
    w_dt,
    w_out,
    attn_gain,
    w_q,
    w_k,
    w_v,
    w_o,
    mlp_gain,
    w_gate,
    w_up,
    w_down,
    dt_bias,
    a_log,
    d_skip,
    conv_x,
    conv_bc,
    inner_gain,
):
    grid = Grid(seq_count)
    via_b, via_e, via_c, via_d = (1, 0, 2), (2, 0, 1), (0, 2, 1), (0, 1, 2)
    rows = w_z.shape[0]
    dt_width = w_dt.shape[1]
    side = jnp.concatenate(
        [
            w_bc.astype(BF),
            w_dt.astype(BF),
            norm_gain.astype(BF)[:, None],
            attn_gain.astype(BF)[:, None],
            mlp_gain.astype(BF)[:, None],
            jnp.zeros((rows, 128 - dt_width - 3), BF),
        ],
        axis=1,
    )
    bc_width = w_bc.shape[1]
    side_all, mark_s = gather_rows(grid, side, via_b)
    x_all, mark_x = gather_rows(grid, w_x.astype(BF), via_c)
    z_all, mark_z = gather_rows(grid, w_z.astype(BF), via_b, mark_x)
    out_all, mark_o = gather_rows(grid, w_out.T.astype(BF), via_e, mark_x)
    qkv = jnp.concatenate([w_q.astype(BF), w_k.astype(BF), w_v.astype(BF)], axis=1)
    qkv_all, mark_q = gather_rows(grid, qkv, via_d, mark_z)
    wo_all, mark_w = gather_rows(grid, w_o.T.astype(BF), via_b, mark_o)
    down_all, mark_d = gather_rows(grid, w_down.T.astype(BF), via_e, mark_q)
    gate_all, mark_g = gather_rows(grid, w_gate.astype(BF), via_b, mark_d)
    up_all, _ = gather_rows(grid, w_up.astype(BF), via_c, mark_g)

    bc_w = side_all[:, :bc_width]
    tail_w = side_all[:, bc_width:]
    dt_w = tail_w[:, :dt_width]
    gains = tail_w[:, dt_width : dt_width + 3].astype(F32).T
    norm_row, attn_row, mlp_row = gains[0], gains[1], gains[2]

    byte_rows = bytes_in.shape[0]
    patch_rows = byte_rows // PATCH
    model_width = bytes_in.shape[1]
    x_float = bytes_in.astype(F32)
    patch_in = jnp.mean(x_float.reshape(patch_rows, PATCH, model_width), axis=1)
    rstd_patch = rms_rows(patch_in)
    h_norm = (patch_in * rstd_patch * norm_row[None, :]).astype(BF)
    inner_local = w_x.shape[1]
    mixed_in = jnp.concatenate([bf_dot(h_norm, x_all), bf_dot(h_norm, bc_w)], axis=1).astype(BF)
    dt_raw = bf_dot(h_norm, dt_w)
    conv_width = conv_x.shape[0]
    state_size = conv_bc.shape[1] // 2
    rim_rows = lax.ppermute(
        mixed_in[patch_rows - (conv_width - 1) :], "seq", [(i, i + 1) for i in range(seq_count - 1)]
    )
    gate_z = bf_dot(h_norm, z_all)
    extended = jnp.concatenate([rim_rows, mixed_in], axis=0).astype(F32)
    first_row = lax.axis_index("seq") * patch_rows
    ids_padded = jnp.concatenate([jnp.full((conv_width - 1,), -1, jnp.int32), seq_ids])
    ids_ext = lax.dynamic_slice_in_dim(ids_padded, first_row, patch_rows + conv_width - 1)
    seg_rows = ids_ext[conv_width - 1 :]
    prev_seg = ids_ext[conv_width - 2]
    head_count = a_log.shape[0]
    head_size = inner_local // head_count

    def mixer_core(ext_in, raw_in, kernel_x, kernel_bc, bias_in, rate_in, skip_in):
        kernel = jnp.concatenate([kernel_x, kernel_bc], axis=1)
        activated = jax.nn.silu(conv_taps(ext_in, ids_ext, kernel))
        x_heads = activated[:, :inner_local].reshape(patch_rows, head_count, head_size)
        b_rows = activated[:, inner_local : inner_local + state_size]
        c_rows = activated[:, inner_local + state_size :]
        step_size = softplus_fn(raw_in + bias_in[None, :])
        log_decay = -step_size * jnp.exp(rate_in)[None, :]
        y_local, decay_in, state_local, total_decay = ssd_block(
            x_heads, b_rows, c_rows, step_size, log_decay, seg_rows, prev_seg, skip_in
        )
        return (y_local, c_rows, decay_in, state_local, total_decay)

    core_out, core_back = jax.vjp(
        mixer_core, extended, dt_raw, conv_x, conv_bc, dt_bias, a_log, d_skip
    )
    y_local, c_rows, decay_in, state_local, total_decay = core_out
    state_in = scan_states(grid, total_decay, state_local, False)[1]

    def finish_mix(y_part, c_part, decay_part, state_part, z_part):
        y_full = y_part + decay_part[:, :, None] * jnp.einsum(
            "tn,hpn->thp", c_part, state_part, precision=PRECISE
        )
        return y_full.reshape(patch_rows, inner_local) * jax.nn.silu(z_part)

    gated_out, finish_back = jax.vjp(finish_mix, y_local, c_rows, decay_in, state_in, gate_z)
    square_sum = mp_sum_exact(jnp.sum(gated_out * gated_out, axis=-1))
    inner_full = inner_local * lax.axis_size("mp")
    rstd_inner = lax.rsqrt(square_sum / inner_full + EPS)[:, None]
    y_norm = (gated_out * rstd_inner * inner_gain[None, :]).astype(BF)
    mixer_out = mp_sum(dot_t(y_norm, out_all))
    patch_out = patch_in + mixer_out
    rows_in = x_float + jnp.repeat(patch_out, PATCH, axis=0)
    rstd_attn = rms_rows(rows_in)
    normed = (rows_in * rstd_attn * attn_row[None, :]).astype(BF)
    attn_width = w_q.shape[1]
    qkv_rows = bf_dot(normed, qkv_all).astype(BF)
    queries = qkv_rows[:, :attn_width]
    key_rows = qkv_rows[:, attn_width : 2 * attn_width]
    value_rows = qkv_rows[:, 2 * attn_width :]
    shape_four = (patch_rows, PATCH, attn_width // LHD, LHD)
    soft_weights = soft_scores(queries, key_rows, shape_four)
    soft_low = soft_weights.astype(BF)
    attended = (
        jnp.einsum(
            "bhqk,bkhd->bqhd",
            soft_low,
            value_rows.reshape(shape_four),
            preferred_element_type=F32,
        )
        .astype(BF)
        .reshape(byte_rows, attn_width)
    )
    after_attn = rows_in + mp_sum(dot_t(attended, wo_all))
    rstd_mlp = rms_rows(after_attn)
    normed_mlp = (after_attn * rstd_mlp * mlp_row[None, :]).astype(BF)
    gate_val = bf_dot(normed_mlp, gate_all)
    up_val = bf_dot(normed_mlp, up_all)
    hidden = (jax.nn.silu(gate_val) * up_val).astype(BF)
    block_out = after_attn + mp_sum(dot_t(hidden, down_all))
    grad_float = out_grad.astype(F32)

    hidden_grad = bf_dot(out_grad, down_all)
    sigmoid_gate = jax.nn.sigmoid(gate_val)
    gate_grad = (
        hidden_grad * up_val * sigmoid_gate * (1.0 + gate_val * (1.0 - sigmoid_gate))
    ).astype(BF)
    up_grad = (hidden_grad * gate_val * sigmoid_gate).astype(BF)
    down_part = grad_dot(out_grad, hidden).astype(BF)
    gate_part = grad_dot(normed_mlp, gate_grad).astype(BF)
    up_part = grad_dot(normed_mlp, up_grad).astype(BF)
    w_down_grad = scatter_rows(grid, down_part, via_e[::-1]).T
    w_gate_grad = scatter_rows(grid, gate_part, via_b[::-1])
    w_up_grad = scatter_rows(grid, up_part, via_c[::-1])
    mlp_norm_grad = mp_sum(dot_t(gate_grad, gate_all) + dot_t(up_grad, up_all))
    mlp_in_grad, mlp_gain_grad = norm_back(mlp_norm_grad, after_attn, rstd_mlp, mlp_row)
    after_grad = grad_float + mlp_in_grad
    after_low = after_grad.astype(BF)
    wo_part = grad_dot(after_low, attended).astype(BF)
    w_o_grad = scatter_rows(grid, wo_part, via_b[::-1]).T
    attended_grad = bf_dot(after_low, wo_all).astype(BF)
    grad_four = attended_grad.reshape(shape_four)
    scale = LHD ** (-0.5)
    prob_grad = jnp.einsum(
        "bqhd,bkhd->bhqk",
        grad_four,
        value_rows.reshape(shape_four),
        preferred_element_type=F32,
    )
    score_grad = (
        soft_weights * (prob_grad - jnp.sum(soft_weights * prob_grad, axis=-1, keepdims=True))
    ).astype(BF)
    query_grad = (
        jnp.einsum(
            "bhqk,bkhd->bqhd",
            score_grad,
            key_rows.reshape(shape_four),
            preferred_element_type=F32,
        )
        * scale
    ).astype(BF)
    key_grad = (
        jnp.einsum(
            "bhqk,bqhd->bkhd",
            score_grad,
            queries.reshape(shape_four),
            preferred_element_type=F32,
        )
        * scale
    ).astype(BF)
    value_grad = jnp.einsum(
        "bhqk,bqhd->bkhd", soft_low, grad_four, preferred_element_type=F32
    ).astype(BF)
    qkv_grad = jnp.concatenate(
        [g.reshape(byte_rows, attn_width) for g in (query_grad, key_grad, value_grad)], axis=1
    )
    qkv_part = grad_dot(normed, qkv_grad).astype(BF)
    w_qkv_grad = scatter_rows(grid, qkv_part, via_d[::-1])
    attn_norm_grad = mp_sum(dot_t(qkv_grad, qkv_all))
    attn_in_grad, attn_gain_grad = norm_back(attn_norm_grad, rows_in, rstd_attn, attn_row)
    rows_grad = after_grad + attn_in_grad
    patch_grad = jnp.sum(rows_grad.reshape(patch_rows, PATCH, model_width), axis=1)
    patch_low = patch_grad.astype(BF)
    out_part = grad_dot(patch_low, y_norm).astype(BF)
    w_out_grad = scatter_rows(grid, out_part, via_e[::-1]).T
    y_norm_grad = bf_dot(patch_low, out_all)
    inner_gain_grad = jnp.sum(y_norm_grad * gated_out * rstd_inner, axis=0)
    scaled = y_norm_grad * inner_gain[None, :]
    cross_sum = mp_sum_exact(jnp.sum(scaled * gated_out, axis=-1))
    gated_grad = rstd_inner * scaled - gated_out * rstd_inner**3 * (cross_sum[:, None] / inner_full)
    y_grad, c_grad, decay_grad, state_in_grad, z_grad = finish_back(gated_grad)
    z_low = z_grad.astype(BF)
    z_part = grad_dot(h_norm, z_low).astype(BF)
    w_z_grad = scatter_rows(grid, z_part, via_b[::-1])
    state_grad = scan_states(grid, total_decay, state_in_grad, True)[1]
    total_grad = jnp.sum(state_grad * state_in, axis=(1, 2))
    ext_grad, raw_grad, conv_x_grad, conv_bc_part, dt_bias_grad, a_log_grad, d_skip_grad = (
        core_back((y_grad, c_grad, decay_grad, state_grad, total_grad))
    )
    bc_total = mp_sum(ext_grad[:, inner_local:])
    conv_bc_grad = mp_sum_exact(conv_bc_part)
    ext_full = jnp.concatenate([ext_grad[:, :inner_local], bc_total], axis=1)
    rim_back = lax.ppermute(
        ext_full[: conv_width - 1], "seq", [(i + 1, i) for i in range(seq_count - 1)]
    )
    mixed_grad = ext_full[conv_width - 1 :] + jnp.concatenate(
        [jnp.zeros((patch_rows - (conv_width - 1), ext_full.shape[1]), F32), rim_back],
        axis=0,
    )
    mixed_low = mixed_grad.astype(BF)
    x_in_grad = mixed_low[:, :inner_local]
    bc_grad = mixed_low[:, inner_local:]
    raw_low = raw_grad.astype(BF)
    x_part = grad_dot(h_norm, x_in_grad).astype(BF)
    w_x_grad = scatter_rows(grid, x_part, via_c[::-1])
    h_own = (
        dot_t(z_low, z_all)
        + dot_t(x_in_grad, x_all)
        + dot_t(raw_low, dt_w)
    )
    h_grad = mp_sum(h_own) + dot_t(bc_grad, bc_w)
    patch_in_grad, norm_gain_grad = norm_back(h_grad, patch_in, rstd_patch, norm_row)
    patch_total = patch_grad + patch_in_grad
    bytes_grad = rows_grad + jnp.repeat(patch_total / PATCH, PATCH, axis=0)
    side_part = jnp.concatenate(
        [
            grad_dot(h_norm, bc_grad),
            grad_dot(h_norm, raw_low),
            norm_gain_grad[:, None],
            attn_gain_grad[:, None],
            mlp_gain_grad[:, None],
            jnp.zeros((model_width, 128 - dt_width - 3), F32),
        ],
        axis=1,
    ).astype(BF)
    side_sum = scatter_rows(grid, side_part, via_b[::-1])
    small = (dt_bias_grad, a_log_grad, d_skip_grad, conv_x_grad, conv_bc_grad, inner_gain_grad)
    flat = jnp.concatenate([s.reshape(-1) for s in small])
    pad = (-flat.shape[0]) % 1024
    flat = seq_sum(jnp.pad(flat, (0, pad)).reshape(-1, 128)).reshape(-1)
    parts = []
    start = 0
    for s in small:
        parts.append(flat[start : start + s.size].reshape(s.shape))
        start += s.size
    return (
        block_out,
        bytes_grad,
        side_sum[:, bc_width + dt_width],
        w_z_grad,
        w_x_grad,
        side_sum[:, :bc_width],
        side_sum[:, bc_width : bc_width + dt_width],
        w_out_grad,
        side_sum[:, bc_width + dt_width + 1],
        w_qkv_grad[:, :attn_width],
        w_qkv_grad[:, attn_width : 2 * attn_width],
        w_qkv_grad[:, 2 * attn_width :],
        w_o_grad,
        side_sum[:, bc_width + dt_width + 2],
        w_gate_grad,
        w_up_grad,
        w_down_grad,
        parts[0],
        parts[1],
        parts[2],
        parts[3],
        parts[4],
        parts[5],
    )


def solution(mesh):
    rows, cols, both, rest = P("seq", None), P("seq", "mp"), P("mp", "seq"), P()
    vec, per = P("seq"), P("mp")
    weights = (vec, cols, cols, rows, cols, both, vec, cols, cols, cols, both, vec, cols, cols, both)
    small = (per, per, per, P(None, "mp"), rest, per)
    in_specs = (rows, rows, rest) + weights + small
    out_specs = (rows, rows) + weights + small
    body = functools.partial(local, mesh.shape["seq"])
    return jax.shard_map(body, mesh=mesh, in_specs=in_specs, out_specs=out_specs, check_vma=False)
```

```python
import functools

import jax
import jax.numpy as jnp
from jax import lax
from jax.experimental import pallas as pl
from jax.experimental.pallas import tpu as pltpu
from jax.sharding import PartitionSpec as P

LHD = 64
PATCH = 8
EPS = 1e-05
BIG = 1e30
PRECISE = lax.Precision.HIGHEST
BF = jnp.bfloat16
F32 = jnp.float32


def factors(count):
    root = 1
    while (root * 2) ** 3 <= count:
        root *= 2
    rest = count // root
    middle = root if rest % root == 0 and rest // root >= root else 1
    return (rest // middle, middle, root)


class Grid:
    def __init__(self, count):
        self.count = count
        self.sizes = factors(count)
        self.place = lax.axis_index("seq")
        n0, n1, n2 = self.sizes
        self.coord = (self.place // (n1 * n2), (self.place // n2) % n1, self.place % n2)

    def pairs(self, dim, by):
        n0, n1, n2 = self.sizes
        out = []
        for i in range(self.count):
            c = [i // (n1 * n2), (i // n2) % n1, i % n2]
            c[dim] = (c[dim] + by) % self.sizes[dim]
            out.append((i, (c[0] * n1 + c[1]) * n2 + c[2]))
        return out

    def shift(self, value, dim, by=1):
        return lax.ppermute(value, "seq", self.pairs(dim, by))


def follow(value, *events):
    return lax.optimization_barrier((value,) + events)[0]


def spread(grid, block, dim, events=()):
    n = grid.sizes[dim]
    me = grid.coord[dim]
    got = [block] + [grid.shift(block, dim, k) for k in range(1, n)]
    if events:
        got = [got[0]] + [follow(g, *events) for g in got[1:]]
    if n == 1:
        return block[None]
    if n == 2:
        first = me == 0
        return jnp.stack([jnp.where(first, got[0], got[1]), jnp.where(first, got[1], got[0])])
    out = jnp.zeros((n,) + block.shape, block.dtype)
    for k, part in enumerate(got):
        out = lax.dynamic_update_index_in_dim(out, part, (me - k) % n, 0)
    return out


def gather_column(grid, block, *events):
    return spread(grid, block, 0, events)


def gather_plane_off(grid, column):
    n0, n1, n2 = grid.sizes
    flat = n1 * n2
    groups = [[z * flat + i for i in range(flat)] for z in range(n0)]
    return lax.all_gather(column, "seq", axis=1, tiled=False, axis_index_groups=groups)


def gather_plane(grid, column):
    n0, n1, n2 = grid.sizes
    _, rows, width = column.shape
    if (n1, n2) != (2, 2) or n0 % 2:
        block = spread(grid, spread(grid, column, 1), 2)
        block = jnp.transpose(block, (2, 1, 0, 3, 4))
        return block.reshape(grid.count * rows, width)
    half = n0 // 2
    parts = (column[:half], column[half:])
    by_x = [grid.shift(p, 2) for p in parts]
    by_y = [grid.shift(p, 1) for p in parts]
    across = [grid.shift(by_x[0], 1), grid.shift(by_y[1], 2)]
    own, by_x, by_y, across = [
        jnp.concatenate(p, axis=0) for p in (parts, by_x, by_y, across)
    ]
    me_y, me_x = grid.coord[1], grid.coord[2]
    tiles = []
    for y in range(2):
        row = []
        for x in range(2):
            same = jnp.where(me_x == x, own, by_x)
            other = jnp.where(me_x == x, by_y, across)
            row.append(jnp.where(me_y == y, same, other))
        tiles.append(jnp.stack(row, axis=1))
    return jnp.stack(tiles, axis=1).reshape(grid.count * rows, width)


def scatter_column(grid, total):
    n = grid.sizes[0]
    me = grid.coord[0]
    total = total.reshape(n, total.shape[0] // n, total.shape[1])
    summed = lax.dynamic_index_in_dim(total, me, 0, False).astype(F32)
    for k in range(1, n):
        block = lax.dynamic_index_in_dim(total, (me + k) % n, 0, False)
        summed = summed + grid.shift(block, 0, k).astype(F32)
    return summed


def scatter_plane(grid, partial):
    n0, n1, n2 = grid.sizes
    flat = n1 * n2
    groups = [[z * flat + i for i in range(flat)] for z in range(n0)]
    return lax.psum_scatter(
        partial, "seq", scatter_dimension=0, tiled=True, axis_index_groups=groups
    )


def scatter_plane_near(grid, partial):
    n0, n1, n2 = grid.sizes
    if (n1, n2) != (2, 2) or n0 % 2:
        return scatter_plane(grid, partial)
    width = partial.shape[1]
    blocks = partial.reshape(4, 2, -1, width)
    me = grid.coord[1] * 2 + grid.coord[2]
    own, by_x, by_y, across = [
        lax.dynamic_index_in_dim(blocks, lax.bitwise_xor(me, k), 0, False) for k in (0, 1, 2, 3)
    ]

    def plus(*terms):
        return sum(t.astype(F32) for t in terms).astype(BF)

    through_y, through_x = grid.shift(across[0], 1), grid.shift(across[1], 2)
    from_x = (grid.shift(plus(by_x[0], through_y), 2), grid.shift(by_x[1], 2))
    from_y = (grid.shift(by_y[0], 1), grid.shift(plus(by_y[1], through_x), 1))
    return jnp.concatenate([plus(own[j], from_x[j], from_y[j]) for j in (0, 1)], axis=0)


def plane_major(grid, values):
    n0, n1, n2 = grid.sizes
    width = values.shape[1]
    rows = width // grid.count
    flat = n1 * n2
    to = lax.broadcasted_iota(jnp.int32, (width, width), 0)
    of = lax.broadcasted_iota(jnp.int32, (width, width), 1)
    plane, z, row = to // (n0 * rows), (to // rows) % n0, to % rows
    pick = ((z * flat + plane) * rows + row == of).astype(BF)
    return rows_rows(pick, values).astype(BF)


def swap_mp(value):
    size = lax.axis_size("mp")
    return lax.ppermute(value, "mp", [(i, (i + 1) % size) for i in range(size)])


def mp_sum(value):
    low = value.astype(BF)
    return low.astype(F32) + swap_mp(low).astype(F32)


def mp_sum_exact(value):
    return value + swap_mp(value)


def seq_sum(value):
    count = lax.axis_size("seq")
    by = 1
    while by < count:
        value = value + lax.ppermute(value, "seq", [(i, i ^ by) for i in range(count)])
        by *= 2
    return value


def spread_small(grid, value):
    for dim in (2, 1, 0):
        n = grid.sizes[dim]
        me = grid.coord[dim]
        got = jnp.stack([value if k == 0 else grid.shift(value, dim, k) for k in range(n)])
        value = jnp.stack([lax.dynamic_index_in_dim(got, (me - j) % n, 0, False) for j in range(n)])
    return value


def scan_states(grid, table, state, reverse, event=None):
    heads = table.shape[-1]
    total = state.reshape(heads, state.shape[0] // heads, state.shape[1])
    enter = jnp.zeros_like(total)
    passed = jnp.ones((heads,), F32)
    levels = [d for d in (2, 1, 0) if grid.sizes[d] > 1]
    crossed = total
    for dim in levels:
        n = grid.sizes[dim]
        me = grid.coord[dim]
        group = table
        for slow in range(dim):
            group = lax.dynamic_index_in_dim(group, grid.coord[slow], 0, False)
        for _ in range(dim + 1, 3):
            group = jnp.prod(group, axis=1)
        index = lax.broadcasted_iota(jnp.int32, (n, 1), 0)

        def product(kept):
            return jnp.prod(jnp.where(kept, group, 1.0), axis=0)

        if event is not None and dim == levels[-1]:
            total = follow(total, event)
        low = total.astype(BF)
        summed = None
        for k in range(n):
            other = (me - k) % n
            ahead = (index < other) if reverse else (index > other)
            before = (index > me) if reverse else (index < me)
            got = total if k == 0 else grid.shift(low, dim, k).astype(F32)
            if k > 0:
                valid = (other > me) if reverse else (other < me)
                weight = jnp.where(valid, product(ahead & before) * passed, 0.0)
                enter = enter + weight[:, None, None] * got
            if dim != levels[-1]:
                term = product(ahead)[:, None, None] * got
                summed = term if summed is None else summed + term
        passed = passed * product((index > me) if reverse else (index < me))
        if dim != levels[-1]:
            crossed = total = summed
    return enter.reshape(state.shape), crossed


VMEM_ROOM = 60 * 2**20
SIDE = 128


def dims(a, b, exact=None):
    return functools.partial(
        lax.dot_general,
        dimension_numbers=(((a,), (b,)), ((), ())),
        precision=exact,
        preferred_element_type=F32,
    )


rows_cols = dims(1, 0)
rows_rows = dims(1, 1)
cols_cols = dims(0, 0)
exact_rc = dims(1, 0, PRECISE)
exact_rr = dims(1, 1, PRECISE)
exact_cc = dims(0, 0, PRECISE)


def call(body, name, shapes, flops, scratch=(), grid=None, in_specs=None, out_specs=None, moved=0):
    kw = {}
    if grid is not None:
        kw = dict(grid=grid, in_specs=in_specs, out_specs=out_specs)
    return pl.pallas_call(
        body,
        out_shape=shapes,
        scratch_shapes=list(scratch),
        name=name,
        compiler_params=pltpu.CompilerParams(vmem_limit_bytes=VMEM_ROOM),
        cost_estimate=pl.CostEstimate(flops=flops, bytes_accessed=moved, transcendentals=0),
        **kw,
    )


def half_lanes(n):
    return lax.broadcasted_iota(jnp.int32, (n, SIDE), 1) < LHD


def two_heads(values, low_half):
    none = jnp.zeros_like(values)
    return jnp.concatenate(
        [jnp.where(low_half, values, none), jnp.where(low_half, none, values)], axis=0
    )


def own_patch(n):
    row = lax.broadcasted_iota(jnp.int32, (n, n), 0)
    col = lax.broadcasted_iota(jnp.int32, (n, n), 1)
    return lax.div(row, PATCH) == lax.div(col, PATCH)


def gathered(values, mine):
    n = values.shape[0]
    kept = jnp.where(mine, values, 0.0).reshape(n // PATCH, PATCH, n)
    return jnp.sum(kept, axis=0)


def widened(values, mine):
    n = mine.shape[0]
    return jnp.where(mine, jnp.concatenate([values] * (n // PATCH), axis=0), 0.0).astype(BF)


def soft_block(scores, mine):
    n = scores.shape[0]
    key = lax.broadcasted_iota(jnp.int32, (PATCH, n), 0)
    query = lax.rem(lax.broadcasted_iota(jnp.int32, (PATCH, n), 1), PATCH)
    block = jnp.where(key <= query, gathered(scores, mine) * (LHD ** (-0.5)), -BIG)
    weights = jnp.exp(block - jnp.max(block, axis=0, keepdims=True))
    return weights / jnp.sum(weights, axis=0, keepdims=True)


def attend_body(width, qkv, out):
    n = qkv.shape[0]
    mine = own_patch(n)
    low_half = half_lanes(n)
    for p in range(width // SIDE):
        at = [slice(j * width + p * SIDE, j * width + (p + 1) * SIDE) for j in range(3)]
        q, k, v = qkv[:, at[0]], qkv[:, at[1]], qkv[:, at[2]]
        scores = rows_rows(two_heads(k, low_half), q)
        soft = [widened(soft_block(scores[j * n : (j + 1) * n], mine), mine) for j in range(2)]
        both = cols_cols(jnp.concatenate(soft, axis=0), two_heads(v, low_half))
        out[:, at[0]] = both.astype(BF)


def attend(qkv):
    rows, three = qkv.shape
    width = three // 3
    return call(
        functools.partial(attend_body, width),
        "attend",
        jax.ShapeDtypeStruct((rows, width), BF),
        rows * SIDE * width * 8,
        grid=(rows // SIDE,),
        in_specs=[pl.BlockSpec((SIDE, three), lambda i: (i, 0))],
        out_specs=pl.BlockSpec((SIDE, width), lambda i: (i, 0)),
        moved=rows * width * 8,
    )(qkv)


def attend_back_body(width, qkv, grad, out):
    n = qkv.shape[0]
    mine = own_patch(n)
    low_half = half_lanes(n)
    scale = LHD ** (-0.5)
    for p in range(width // SIDE):
        at = [slice(j * width + p * SIDE, j * width + (p + 1) * SIDE) for j in range(3)]
        q, k, v = qkv[:, at[0]], qkv[:, at[1]], qkv[:, at[2]]
        g = grad[:, at[0]]
        k_two = two_heads(k, low_half)
        scores = rows_rows(k_two, q)
        probs = rows_rows(two_heads(v, low_half), g)
        soft_wide, back_wide = [], []
        for j in range(2):
            rows = slice(j * n, (j + 1) * n)
            soft = soft_block(scores[rows], mine)
            prob = gathered(probs[rows], mine)
            back = soft * (prob - jnp.sum(soft * prob, axis=0, keepdims=True))
            soft_wide.append(widened(soft, mine))
            back_wide.append(widened(back, mine))
        q_grad = cols_cols(jnp.concatenate(back_wide, axis=0), k_two)
        k_grad = rows_cols(jnp.concatenate(back_wide, axis=1), two_heads(q, low_half))
        v_grad = rows_cols(jnp.concatenate(soft_wide, axis=1), two_heads(g, low_half))
        out[:, at[0]] = (q_grad * scale).astype(BF)
        out[:, at[1]] = (k_grad * scale).astype(BF)
        out[:, at[2]] = v_grad.astype(BF)


def attend_back(qkv, grad):
    rows, three = qkv.shape
    width = three // 3
    return call(
        functools.partial(attend_back_body, width),
        "attend_back",
        jax.ShapeDtypeStruct((rows, three), BF),
        rows * SIDE * width * 20,
        grid=(rows // SIDE,),
        in_specs=[
            pl.BlockSpec((SIDE, three), lambda i: (i, 0)),
            pl.BlockSpec((SIDE, width), lambda i: (i, 0)),
        ],
        out_specs=pl.BlockSpec((SIDE, three), lambda i: (i, 0)),
        moved=rows * width * 14,
    )(qkv, grad)


def middle_body(step, normed, grad, w_down, w_pair, hidden, pair):
    x = normed[...]
    gate = rows_cols(x, w_pair[:, :step])
    up = rows_cols(x, w_pair[:, step:])
    back = rows_cols(grad[...], w_down[...])
    sig = 1.0 / (1.0 + jnp.exp(-gate))
    act = gate * sig
    hidden[...] = (act * up).astype(BF)
    pair[:, step:] = (back * act).astype(BF)
    pair[:, :step] = (back * up * sig * (1.0 + gate * (1.0 - sig))).astype(BF)


def middle(normed, grad, w_all, ff, step):
    rows, width = normed.shape
    return call(
        functools.partial(middle_body, step),
        "middle",
        (jax.ShapeDtypeStruct((rows, ff), BF), jax.ShapeDtypeStruct((rows, 2 * ff), BF)),
        rows * width * ff * 6,
        grid=(ff // step,),
        in_specs=[
            pl.BlockSpec((rows, width), lambda i: (0, 0)),
            pl.BlockSpec((rows, width), lambda i: (0, 0)),
            pl.BlockSpec((width, step), lambda i: (0, i)),
            pl.BlockSpec((width, 2 * step), lambda i: (0, i + ff // (2 * step))),
        ],
        out_specs=(
            pl.BlockSpec((rows, step), lambda i: (0, i)),
            pl.BlockSpec((rows, 2 * step), lambda i: (0, i)),
        ),
        moved=rows * width * 4 + width * ff * 6 + rows * ff * 6,
    )(normed, grad, w_all, w_all)


def products_body(starts, *refs):
    count = len(starts) - 1
    out = refs[2 * count]
    for j in range(count):

        @pl.when((pl.program_id(0) >= starts[j]) & (pl.program_id(0) < starts[j + 1]))
        def _(j=j):
            out[...] = rows_cols(refs[2 * j][...], refs[2 * j + 1][...]).astype(out.dtype)


def products(pairs, step):
    starts = [0]
    in_specs, args, flops, moved = [], [], 0, 0
    for left, right in pairs:
        first, runs = starts[-1], right.shape[1] // step
        starts.append(first + runs)
        in_specs.append(pl.BlockSpec(left.shape, lambda i: (0, 0)))

        def column(i, first=first, runs=runs):
            return (0, jnp.clip(i - first, 0, runs - 1))

        in_specs.append(pl.BlockSpec((right.shape[0], step), column))
        args += [left, right]
        flops += 2 * left.shape[0] * right.shape[0] * right.shape[1]
        moved += 2 * (left.size + right.size)
    m = pairs[0][0].shape[0]
    return call(
        functools.partial(products_body, tuple(starts)),
        "products",
        jax.ShapeDtypeStruct((m, starts[-1] * step), BF),
        flops,
        grid=(starts[-1],),
        in_specs=in_specs,
        out_specs=pl.BlockSpec((m, step), lambda i: (0, i)),
        moved=moved + 2 * m * starts[-1] * step,
    )(*args)


def softplus_fn(values):
    return jnp.log1p(jnp.exp(-jnp.abs(values))) + jnp.maximum(values, 0.0)


def lower_ones(n):
    row = lax.broadcasted_iota(jnp.int32, (n, n), 0)
    col = lax.broadcasted_iota(jnp.int32, (n, n), 1)
    return row >= col


def taps_fill(rim, mixed, buf, taps):
    buf[0:8, :] = rim[...].astype(F32)
    buf[8 : 8 + mixed.shape[0], :] = mixed[...].astype(F32)


def conv_here(buf, k_x, k_bc, info, n, taps):
    wide = jnp.concatenate([k_x[...], k_bc[...]], axis=1)
    total = None
    for k in range(taps):
        at = 9 - taps + k
        term = buf[at : at + n, :] * wide[k : k + 1, :] * info[:, k : k + 1]
        total = term if total is None else total + term
    return total


def decays(raw, small, n):
    base = raw[...] + small[0:1, :]
    step = softplus_fn(base)
    rate = jnp.exp(small[1:2, :])
    log_decay = -step * rate
    tri = lower_ones(n).astype(F32)
    cum = exact_rc(tri, log_decay)
    return base, step, rate, log_decay, tri, cum


def mix_body(taps, inner, rim, mixed, raw, small, skip, k_x, k_bc, info, seg, y_out, c_out, din_out, state_out, buf):
    n = mixed.shape[0]
    taps_fill(rim, mixed, buf, taps)
    pre = conv_here(buf, k_x, k_bc, info, n, taps)
    act = pre / (1.0 + jnp.exp(-pre))
    b = act[:, inner : inner + SIDE]
    c = act[:, inner + SIDE :]
    _, step, _, _, _, cum = decays(raw, small, n)
    cum_t, step_t = cum.T, step.T
    live = lower_ones(n) & (info[:, 6:7] == seg[0:1, :])
    both = exact_rr(c, b)
    din_out[...] = info[:, 4:5] * jnp.exp(cum)
    tail = jnp.exp(jnp.where(info[:, 5:6] > 0.0, cum[n - 1 : n, :] - cum, -BIG)) * step
    low_half = half_lanes(n)
    c_out[...] = c
    for p in range(inner // SIDE):
        at = slice(p * SIDE, (p + 1) * SIDE)
        x = act[:, at]
        y = skip[0:1, at] * x
        for j, mine in enumerate((low_half, ~low_half)):
            h = 2 * p + j
            gaps = jnp.exp(jnp.where(live, cum[:, h : h + 1] - cum_t[h : h + 1, :], -BIG))
            mix = both * gaps * step_t[h : h + 1, :]
            y = y + exact_rc(mix, jnp.where(mine, x, 0.0))
        y_out[:, at] = y
        weighted = x * jnp.where(low_half, tail[:, 2 * p : 2 * p + 1], tail[:, 2 * p + 1 : 2 * p + 2])
        state_out[at, :] = exact_cc(weighted, b)


def mix(rim, mixed, raw, small, skip, k_x, k_bc, info, seg):
    n, wide = mixed.shape
    taps, inner = k_x.shape
    return call(
        functools.partial(mix_body, taps, inner),
        "mix",
        (
            jax.ShapeDtypeStruct((n, inner), F32),
            jax.ShapeDtypeStruct((n, SIDE), F32),
            jax.ShapeDtypeStruct((n, SIDE), F32),
            jax.ShapeDtypeStruct((inner, SIDE), F32),
        ),
        n * n * inner * 24,
        scratch=(pltpu.VMEM((n + 8, wide), F32),),
        moved=n * inner * 20,
    )(rim, mixed, raw, small, skip, k_x, k_bc, info, seg)


def pair_cols(values, p, low_half):
    return jnp.where(low_half, values[:, 2 * p : 2 * p + 1], values[:, 2 * p + 1 : 2 * p + 2])


def finish_body(inner, y_part, c, din, state, z, y_out, gated_out, square):
    n = y_part.shape[0]
    low_half = half_lanes(n)
    total = None
    for p in range(inner // SIDE):
        at = slice(p * SIDE, (p + 1) * SIDE)
        y = y_part[:, at] + pair_cols(din, p, low_half) * exact_rr(c[...], state[at, :])
        gate = z[:, at]
        gated = y * (gate / (1.0 + jnp.exp(-gate)))
        y_out[:, at] = y
        gated_out[:, at] = gated
        term = gated * gated
        total = term if total is None else total + term
    square[...] = jnp.broadcast_to(jnp.sum(total, axis=1, keepdims=True), square.shape)


def finish(y_part, c, din, state, z):
    n, inner = y_part.shape
    return call(
        functools.partial(finish_body, inner),
        "finish",
        (
            jax.ShapeDtypeStruct((n, inner), F32),
            jax.ShapeDtypeStruct((n, inner), F32),
            jax.ShapeDtypeStruct((n, SIDE), F32),
        ),
        n * SIDE * inner * 12,
        moved=n * inner * 20,
    )(y_part, c, din, state, z)


def unfinish_body(inner, y_norm_grad, gated, y_full, z, gain, stats, din, c, y_grad, z_grad, state_grad):
    n = gated.shape[0]
    low_half = half_lanes(n)
    for p in range(inner // SIDE):
        at = slice(p * SIDE, (p + 1) * SIDE)
        back = stats[:, 0:1] * (y_norm_grad[:, at] * gain[0:1, at]) - gated[:, at] * stats[:, 1:2]
        gate = z[:, at]
        sig = 1.0 / (1.0 + jnp.exp(-gate))
        y_back = back * gate * sig
        y_grad[:, at] = y_back
        z_grad[:, at] = (back * y_full[:, at] * sig * (1.0 + gate * (1.0 - sig))).astype(BF)
        state_grad[at, :] = exact_cc(y_back * pair_cols(din, p, low_half), c[...])


def unfinish(y_norm_grad, gated, y_full, z, gain, stats, din, c):
    n, inner = gated.shape
    return call(
        functools.partial(unfinish_body, inner),
        "unfinish",
        (
            jax.ShapeDtypeStruct((n, inner), F32),
            jax.ShapeDtypeStruct((n, inner), BF),
            jax.ShapeDtypeStruct((inner, SIDE), F32),
        ),
        n * SIDE * inner * 12,
        moved=n * inner * 24,
    )(y_norm_grad, gated, y_full, z, gain, stats, din, c)


def unmix_body(
    taps, inner, rim, mixed, raw, small, skip, k_x, k_bc, info, seg, y_grad, state_in, state_back,
    ext_out, raw_out, taps_out, heads_out, skip_out, buf, d_buf, d_act, cols, sums, steps,
):
    n = mixed.shape[0]
    taps_fill(rim, mixed, buf, taps)
    pre = conv_here(buf, k_x, k_bc, info, n, taps)
    sig_pre = 1.0 / (1.0 + jnp.exp(-pre))
    act = pre * sig_pre
    b = act[:, inner : inner + SIDE]
    c = act[:, inner + SIDE :]
    base, step, rate, log_decay, tri, cum = decays(raw, small, n)
    cum_t, step_t = cum.T, step.T
    live = lower_ones(n) & (info[:, 6:7] == seg[0:1, :])
    both = exact_rr(c, b)
    din = info[:, 4:5] * jnp.exp(cum)
    tail = jnp.exp(jnp.where(info[:, 5:6] > 0.0, cum[n - 1 : n, :] - cum, -BIG))
    low_half = half_lanes(n)
    cols[...] = jnp.zeros_like(cols)
    sums[...] = jnp.zeros_like(sums)
    steps[...] = jnp.zeros_like(steps)
    both_grad = jnp.zeros((n, n), F32)
    b_grad = jnp.zeros((n, SIDE), F32)
    c_grad = jnp.zeros((n, SIDE), F32)
    lane = lax.broadcasted_iota(jnp.int32, (1, SIDE), 1)
    total_grad = jnp.zeros((1, SIDE), F32)
    tail_grad = jnp.zeros((n, SIDE), F32)
    for p in range(inner // SIDE):
        at = slice(p * SIDE, (p + 1) * SIDE)
        x = act[:, at]
        dy = y_grad[:, at]
        s_in = state_in[at, :]
        s_back = state_back[at, :]
        out_b = exact_rr(b, s_back)
        weight = pair_cols(tail, p, low_half) * pair_cols(step, p, low_half)
        dx = skip[0:1, at] * dy + weight * out_b
        b_grad = b_grad + exact_rc(x * weight, s_back)
        dy_in = pair_cols(din, p, low_half) * dy
        in_c = exact_rr(c, s_in)
        c_grad = c_grad + exact_rc(dy_in, s_in)
        skip_out[0:1, at] = jnp.sum(dy * x, axis=0, keepdims=True)
        held = jnp.sum(s_in * s_back, axis=1, keepdims=True)
        for j, mine in enumerate((low_half, ~low_half)):
            h = 2 * p + j
            dy_mine = jnp.where(mine, dy, 0.0)
            gaps = jnp.exp(jnp.where(live, cum[:, h : h + 1] - cum_t[h : h + 1, :], -BIG))
            step_row = step_t[h : h + 1, :]
            back = exact_rr(dy_mine, x) * gaps
            both_grad = both_grad + back * step_row
            back = back * both
            each = back * step_row
            dx = dx + exact_cc(both * gaps * step_row, dy_mine)
            steps[h : h + 1, :] = jnp.sum(back, axis=0, keepdims=True)
            sums[h : h + 1, :] = -jnp.sum(each, axis=0, keepdims=True)
            from_in = jnp.sum(jnp.where(mine, dy_in * in_c, 0.0), axis=1, keepdims=True)
            cols[:, h : h + 1] = jnp.sum(each, axis=1, keepdims=True) + from_in
            from_tail = jnp.sum(jnp.where(mine, x * out_b, 0.0), axis=1, keepdims=True)
            tail_grad = tail_grad + jnp.where(lane == h, from_tail, 0.0)
            here = jnp.sum(held[j * LHD : (j + 1) * LHD, :], axis=0, keepdims=True)
            total_grad = total_grad + jnp.where(lane == h, here, 0.0)
        d_act[:, at] = dx
    d_act[:, inner : inner + SIDE] = b_grad + exact_cc(both_grad, c)
    d_act[:, inner + SIDE :] = c_grad + exact_rc(both_grad, b)
    tail_back = tail_grad * tail
    row = lax.broadcasted_iota(jnp.int32, (n, SIDE), 0)
    moved = tail_back * step
    last = jnp.sum(moved, axis=0, keepdims=True) + total_grad * din[n - 1 : n, :]
    cum_grad = cols[...] + sums[...].T - moved + jnp.where(row == n - 1, last, 0.0)
    decay_grad = exact_cc(tri, cum_grad)
    step_grad = steps[...].T + tail_back - decay_grad * rate
    raw_grad = step_grad / (1.0 + jnp.exp(-base))
    raw_out[...] = raw_grad
    heads_out[0:1, :] = jnp.sum(raw_grad, axis=0, keepdims=True)
    heads_out[1:2, :] = jnp.sum(decay_grad * log_decay, axis=0, keepdims=True)
    heads_out[2:8, :] = jnp.zeros((6, SIDE), F32)
    d_pre = d_act[...] * (sig_pre * (1.0 + pre * (1.0 - sig_pre)))
    d_buf[...] = jnp.zeros_like(d_buf)
    wide = jnp.concatenate([k_x[...], k_bc[...]], axis=1)
    for k in range(taps):
        at = 9 - taps + k
        masked = d_pre * info[:, k : k + 1]
        d_buf[at : at + n, :] = d_buf[at : at + n, :] + masked * wide[k : k + 1, :]
        taps_out[k : k + 1, :] = jnp.sum(masked * buf[at : at + n, :], axis=0, keepdims=True)
    ext_out[...] = d_buf[...]


def unmix(rim, mixed, raw, small, skip, k_x, k_bc, info, seg, y_grad, state_in, state_back):
    n, wide = mixed.shape
    taps, inner = k_x.shape
    return call(
        functools.partial(unmix_body, taps, inner),
        "unmix",
        (
            jax.ShapeDtypeStruct((n + 8, wide), F32),
            jax.ShapeDtypeStruct((n, SIDE), F32),
            jax.ShapeDtypeStruct((taps, wide), F32),
            jax.ShapeDtypeStruct((8, SIDE), F32),
            jax.ShapeDtypeStruct((1, inner), F32),
        ),
        n * n * inner * 96,
        scratch=(
            pltpu.VMEM((n + 8, wide), F32),
            pltpu.VMEM((n + 8, wide), F32),
            pltpu.VMEM((n, wide), F32),
            pltpu.VMEM((n, SIDE), F32),
            pltpu.VMEM((SIDE, n), F32),
            pltpu.VMEM((SIDE, n), F32),
        ),
        moved=n * inner * 30,
    )(rim, mixed, raw, small, skip, k_x, k_bc, info, seg, y_grad, state_in, state_back)


def bf_dot(left, right):
    return rows_cols(left, right)


def dot_t(left, right):
    return rows_rows(left, right)


def grad_dot(left, right):
    return cols_cols(left, right)


def rms_rows(values):
    return lax.rsqrt(jnp.mean(values * values, axis=-1, keepdims=True) + EPS)


def norm_back(grad_in, values, rstd_rows, gain_row):
    normed_rows = values * rstd_rows
    gain_grad = jnp.sum(grad_in * normed_rows, axis=0)
    scaled = grad_in * gain_row[None, :]
    input_grad = rstd_rows * (
        scaled - normed_rows * jnp.mean(scaled * normed_rows, axis=-1, keepdims=True)
    )
    return (input_grad, gain_grad)


def local(
    seq_count,
    bytes_in,
    out_grad,
    seq_ids,
    norm_gain,
    w_z,
    w_x,
    w_bc,
    w_dt,
    w_out,
    attn_gain,
    w_q,
    w_k,
    w_v,
    w_o,
    mlp_gain,
    w_gate,
    w_up,
    w_down,
    dt_bias,
    a_log,
    d_skip,
    conv_x,
    conv_bc,
    inner_gain,
):
    grid = Grid(seq_count)
    rows, ff = w_gate.shape
    inner = w_x.shape[1]
    bc_width = w_bc.shape[1]
    heads = w_dt.shape[1]
    attn_width = w_q.shape[1]
    step = min(256, ff)
    byte_rows, model_width = bytes_in.shape
    patch_rows = byte_rows // PATCH
    taps = conv_x.shape[0]
    inner_full = inner * lax.axis_size("mp")

    first = jnp.concatenate(
        [
            w_x.astype(BF),
            w_bc.astype(BF),
            w_dt.astype(BF),
            norm_gain.astype(BF)[:, None],
            attn_gain.astype(BF)[:, None],
            mlp_gain.astype(BF)[:, None],
            jnp.zeros((rows, SIDE - heads - 3), BF),
        ],
        axis=1,
    )
    first_column = gather_column(grid, first)
    first_all = gather_plane(grid, first_column)
    second = jnp.concatenate(
        [w.astype(BF) for w in (w_z, w_out.T, w_q, w_k, w_v, w_o.T)], axis=1
    )
    second = follow(second, first_column)
    pair = jnp.stack(
        [w.astype(BF).reshape(rows, ff // step, step) for w in (w_gate, w_up)], axis=2
    ).reshape(rows, 2 * ff)
    mlp = jnp.concatenate([w_down.T.astype(BF), pair], axis=1)

    tail_all = first_all[:, inner + bc_width :]
    gains = tail_all[:, heads : heads + 3].astype(F32).T
    norm_row, attn_row, mlp_row = gains[0], gains[1], gains[2]
    x_float = bytes_in.astype(F32)
    patch_in = jnp.mean(x_float.reshape(patch_rows, PATCH, model_width), axis=1)
    rstd_patch = rms_rows(patch_in)
    h_norm = (patch_in * rstd_patch * norm_row[None, :]).astype(BF)
    into = bf_dot(h_norm, first_all)
    mixed = into[:, : inner + bc_width].astype(BF)
    raw = into[:, inner + bc_width :]
    second_column = gather_column(grid, second, mixed)
    second_all = gather_plane_off(grid, second_column).reshape(model_width, -1)
    z_all, out_all = second_all[:, :inner], second_all[:, inner : 2 * inner]
    third_all = second_all[:, 2 * inner :]
    qkv_all, wo_all = third_all[:, : 3 * attn_width], third_all[:, 3 * attn_width :]
    rim = lax.ppermute(
        mixed[patch_rows - (taps - 1) :], "seq", [(i, i + 1) for i in range(seq_count - 1)]
    )
    rim = jnp.pad(rim, ((8 - (taps - 1), 0), (0, 0)))
    first_row = lax.axis_index("seq") * patch_rows
    ids_padded = jnp.concatenate([jnp.full((taps - 1,), -1, jnp.int32), seq_ids])
    ids_ext = lax.dynamic_slice_in_dim(ids_padded, first_row, patch_rows + taps - 1)
    ids = ids_ext[taps - 1 :]
    columns = [ids_ext[k : k + patch_rows] == ids for k in range(taps)]
    columns += [ids == ids_ext[taps - 2], ids == ids[patch_rows - 1], ids]
    info = jnp.stack([c.astype(F32) for c in columns], axis=1)
    info = jnp.pad(info, ((0, 0), (0, SIDE - info.shape[1])))
    seg = jnp.broadcast_to(ids.astype(F32)[None, :], (8, patch_rows))
    small = jnp.pad(jnp.stack([dt_bias, a_log]), ((0, 6), (0, SIDE - heads)))
    skip = jnp.repeat(d_skip, inner // heads)[None, :]
    whole = jnp.sum(softplus_fn(raw[:, :heads] + dt_bias), axis=0) * -jnp.exp(a_log)
    table = spread_small(grid, info[patch_rows - 1, taps] * jnp.exp(whole))
    known = (rim, mixed, raw, small, skip, conv_x, conv_bc, info, seg)
    y_part, c_rows, decay_in, state_own = mix(*known)
    state_in, crossed = scan_states(grid, table, state_own, False)
    mlp_column = gather_column(grid, follow(mlp, first_all, second_column), crossed)
    mlp_all = gather_plane_off(grid, follow(mlp_column, second_all)).reshape(model_width, -1)
    down_all, pair_all = mlp_all[:, :ff], mlp_all[:, ff:]
    gate_z = bf_dot(h_norm, z_all)
    y_full, gated, square = finish(y_part, c_rows, decay_in, state_in, gate_z)
    square_sum = mp_sum_exact(square[:, 0])
    rstd_inner = lax.rsqrt(square_sum / inner_full + EPS)[:, None]
    y_norm = (gated * rstd_inner * inner_gain[None, :]).astype(BF)
    mixer_out = mp_sum(dot_t(y_norm, out_all))
    patch_out = patch_in + mixer_out

    rows_in = x_float + jnp.repeat(patch_out, PATCH, axis=0)
    rstd_attn = rms_rows(rows_in)
    normed = (rows_in * rstd_attn * attn_row[None, :]).astype(BF)
    qkv = bf_dot(normed, qkv_all).astype(BF)
    attended = attend(qkv)
    after_attn = rows_in + mp_sum(dot_t(attended, wo_all))
    rstd_mlp = rms_rows(after_attn)
    normed_mlp = (after_attn * rstd_mlp * mlp_row[None, :]).astype(BF)
    hidden, pair_grad = middle(normed_mlp, out_grad, mlp_all, ff, step)
    block_out = after_attn + mp_sum(dot_t(hidden, down_all))

    mlp_part = products(
        (
            (plane_major(grid, normed_mlp), pair_grad),
            (plane_major(grid, out_grad), hidden),
        ),
        2 * step,
    )
    mlp_plane = scatter_plane(grid, mlp_part)
    pair_grad = follow(pair_grad, mlp_part)
    mlp_norm_grad = mp_sum(dot_t(pair_grad, pair_all))
    mlp_in_grad, mlp_gain_grad = norm_back(mlp_norm_grad, after_attn, rstd_mlp, mlp_row)
    after_grad = out_grad.astype(F32) + mlp_in_grad
    after_low = after_grad.astype(BF)
    attended_grad = bf_dot(after_low, wo_all).astype(BF)
    qkv_grad = attend_back(qkv, attended_grad)
    third_part = products(
        (
            (plane_major(grid, normed), qkv_grad),
            (plane_major(grid, after_low), attended),
        ),
        attn_width,
    )
    qkv_grad = follow(qkv_grad, third_part)
    attn_norm_grad = mp_sum(dot_t(qkv_grad, qkv_all))
    attn_in_grad, attn_gain_grad = norm_back(attn_norm_grad, rows_in, rstd_attn, attn_row)
    rows_grad = after_grad + attn_in_grad
    patch_grad = jnp.sum(rows_grad.reshape(patch_rows, PATCH, model_width), axis=1)
    patch_low = patch_grad.astype(BF)
    y_norm_grad = bf_dot(patch_low, out_all)
    shared = y_norm_grad * gated
    inner_gain_grad = jnp.sum(shared * rstd_inner, axis=0)
    cross_sum = mp_sum_exact(jnp.sum(shared * inner_gain[None, :], axis=-1))[:, None]
    stats = jnp.concatenate([rstd_inner, rstd_inner**3 * (cross_sum / inner_full)], axis=1)
    stats = jnp.pad(stats, ((0, 0), (0, SIDE - 2)))
    y_grad, z_low, state_in_grad = unfinish(
        y_norm_grad, gated, y_full, gate_z, inner_gain[None, :], stats, decay_in, c_rows
    )
    h_norm_t = plane_major(grid, h_norm)
    second_part = products(((h_norm_t, z_low), (plane_major(grid, patch_low), y_norm)), inner)
    state_in_grad = follow(state_in_grad, second_part)
    state_grad, crossed = scan_states(grid, table, state_in_grad, True, mlp_plane)
    third_plane = scatter_plane(grid, follow(third_part, mlp_plane, crossed))
    ext_grad, raw_grad, taps_grad, heads_grad, skip_grad = unmix(
        *known, y_grad, state_in, state_grad
    )
    bc_total = mp_sum(ext_grad[:, inner:])
    conv_bc_grad = mp_sum_exact(taps_grad[:, inner:])
    ext_full = jnp.concatenate([ext_grad[:, :inner], bc_total], axis=1)
    rim_back = lax.ppermute(
        ext_full[8 - (taps - 1) : 8], "seq", [(i + 1, i) for i in range(seq_count - 1)]
    )
    mixed_low = (
        ext_full[8:] + jnp.pad(rim_back, ((patch_rows - (taps - 1), 0), (0, 0)))
    ).astype(BF)
    first_grad = jnp.concatenate([mixed_low, raw_grad.astype(BF)], axis=1)
    first_part = bf_dot(h_norm_t, first_grad).astype(BF)
    first_grad = follow(first_grad, first_part)
    second_plane = scatter_plane(grid, follow(second_part, third_plane, first_part))
    first_plane = scatter_plane_near(grid, first_part)
    lane = lax.broadcasted_iota(jnp.int32, (1, first_grad.shape[1]), 1)
    twice = (lane >= inner) & (lane < inner + bc_width) & (lax.axis_index("mp") > 0)
    own_grad = jnp.where(twice, jnp.zeros_like(first_grad), first_grad)
    h_grad = mp_sum(dot_t(own_grad, first_all) + dot_t(z_low, z_all))
    patch_in_grad, norm_gain_grad = norm_back(h_grad, patch_in, rstd_patch, norm_row)
    patch_total = patch_grad + patch_in_grad
    bytes_grad = rows_grad + jnp.repeat(patch_total / PATCH, PATCH, axis=0)

    mlp_sum = scatter_column(grid, follow(mlp_plane, state_grad))
    pair_sum = mlp_sum[:, : 2 * ff].reshape(rows, ff // step, 2, step)
    w_gate_grad = pair_sum[:, :, 0].reshape(rows, ff)
    w_up_grad = pair_sum[:, :, 1].reshape(rows, ff)
    w_down_grad = mlp_sum[:, 2 * ff :].T
    third_sum = scatter_column(grid, third_plane)
    w_qkv_grad, w_o_grad = third_sum[:, : 3 * attn_width], third_sum[:, 3 * attn_width :].T
    second_sum = scatter_column(grid, second_plane)
    w_z_grad, w_out_grad = second_sum[:, :inner], second_sum[:, inner:].T
    first_sum = scatter_column(grid, first_plane)

    pieces = (
        heads_grad[:2],
        skip_grad,
        taps_grad[:, :inner],
        conv_bc_grad,
        inner_gain_grad,
        norm_gain_grad,
        attn_gain_grad,
        mlp_gain_grad,
    )
    flat = seq_sum(jnp.concatenate([p.reshape(-1, SIDE) for p in pieces], axis=0))
    parts, start = [], 0
    for p in pieces:
        stop = start + p.size // SIDE
        parts.append(flat[start:stop].reshape(p.shape))
        start = stop
    mine = lax.axis_index("seq") * rows
    gain_parts = [lax.dynamic_slice_in_dim(g, mine, rows) for g in parts[5:]]
    return (
        block_out,
        bytes_grad,
        gain_parts[0],
        w_z_grad,
        first_sum[:, :inner],
        first_sum[:, inner : inner + bc_width],
        first_sum[:, inner + bc_width : inner + bc_width + heads],
        w_out_grad,
        gain_parts[1],
        w_qkv_grad[:, :attn_width],
        w_qkv_grad[:, attn_width : 2 * attn_width],
        w_qkv_grad[:, 2 * attn_width :],
        w_o_grad,
        gain_parts[2],
        w_gate_grad,
        w_up_grad,
        w_down_grad,
        parts[0][0, :heads],
        parts[0][1, :heads],
        jnp.sum(parts[1].reshape(heads, inner // heads), axis=1),
        parts[2],
        parts[3],
        parts[4],
    )


def solution(mesh):
    rows, cols, both, rest = P("seq", None), P("seq", "mp"), P("mp", "seq"), P()
    vec, per = P("seq"), P("mp")
    weights = (vec, cols, cols, rows, cols, both, vec, cols, cols, cols, both, vec, cols, cols, both)
    small = (per, per, per, P(None, "mp"), rest, per)
    in_specs = (rows, rows, rest) + weights + small
    out_specs = (rows, rows) + weights + small
    body = functools.partial(local, mesh.shape["seq"])
    return jax.shard_map(body, mesh=mesh, in_specs=in_specs, out_specs=out_specs, check_vma=False)
```

```python
import functools

import jax
import jax.numpy as jnp
from jax import lax
from jax.experimental import pallas as pl
from jax.experimental.pallas import tpu as pltpu
from jax.sharding import PartitionSpec as P

LHD = 64
PATCH = 8
EPS = 1e-05
BIG = 1e30
PRECISE = lax.Precision.HIGHEST
BF = jnp.bfloat16
F32 = jnp.float32


def factors(count):
    root = 1
    while (root * 2) ** 3 <= count:
        root *= 2
    rest = count // root
    middle = root if rest % root == 0 and rest // root >= root else 1
    return (rest // middle, middle, root)


class Grid:
    def __init__(self, count):
        self.count = count
        self.sizes = factors(count)
        self.place = lax.axis_index("seq")
        n0, n1, n2 = self.sizes
        self.coord = (self.place // (n1 * n2), (self.place // n2) % n1, self.place % n2)

    def pairs(self, dim, by):
        n0, n1, n2 = self.sizes
        out = []
        for i in range(self.count):
            c = [i // (n1 * n2), (i // n2) % n1, i % n2]
            c[dim] = (c[dim] + by) % self.sizes[dim]
            out.append((i, (c[0] * n1 + c[1]) * n2 + c[2]))
        return out

    def shift(self, value, dim, by=1):
        return lax.ppermute(value, "seq", self.pairs(dim, by))


def follow(value, *events):
    return lax.optimization_barrier((value,) + events)[0]


def spread(grid, block, dim, events=()):
    n = grid.sizes[dim]
    me = grid.coord[dim]
    got = [block] + [grid.shift(block, dim, k) for k in range(1, n)]
    if events:
        got = [got[0]] + [follow(g, *events) for g in got[1:]]
    if n == 1:
        return block[None]
    if n == 2:
        first = me == 0
        return jnp.stack([jnp.where(first, got[0], got[1]), jnp.where(first, got[1], got[0])])
    out = jnp.zeros((n,) + block.shape, block.dtype)
    for k, part in enumerate(got):
        out = lax.dynamic_update_index_in_dim(out, part, (me - k) % n, 0)
    return out


def gather_column(grid, block, *events):
    return spread(grid, block, 0, events)


def gather_plane_off(grid, column):
    n0, n1, n2 = grid.sizes
    flat = n1 * n2
    groups = [[z * flat + i for i in range(flat)] for z in range(n0)]
    return lax.all_gather(column, "seq", axis=1, tiled=False, axis_index_groups=groups)


def gather_plane(grid, column):
    n0, n1, n2 = grid.sizes
    _, rows, width = column.shape
    if (n1, n2) != (2, 2) or n0 % 2:
        block = spread(grid, spread(grid, column, 1), 2)
        block = jnp.transpose(block, (2, 1, 0, 3, 4))
        return block.reshape(grid.count * rows, width)
    half = n0 // 2
    parts = (column[:half], column[half:])
    by_x = [grid.shift(p, 2) for p in parts]
    by_y = [grid.shift(p, 1) for p in parts]
    across = [grid.shift(by_x[0], 1), grid.shift(by_y[1], 2)]
    own, by_x, by_y, across = [
        jnp.concatenate(p, axis=0) for p in (parts, by_x, by_y, across)
    ]
    me_y, me_x = grid.coord[1], grid.coord[2]
    tiles = []
    for y in range(2):
        row = []
        for x in range(2):
            same = jnp.where(me_x == x, own, by_x)
            other = jnp.where(me_x == x, by_y, across)
            row.append(jnp.where(me_y == y, same, other))
        tiles.append(jnp.stack(row, axis=1))
    return jnp.stack(tiles, axis=1).reshape(grid.count * rows, width)


def scatter_column(grid, total):
    n = grid.sizes[0]
    me = grid.coord[0]
    total = total.reshape(n, total.shape[0] // n, total.shape[1])
    summed = lax.dynamic_index_in_dim(total, me, 0, False).astype(F32)
    for k in range(1, n):
        block = lax.dynamic_index_in_dim(total, (me + k) % n, 0, False)
        summed = summed + grid.shift(block, 0, k).astype(F32)
    return summed


def scatter_plane(grid, partial):
    n0, n1, n2 = grid.sizes
    flat = n1 * n2
    groups = [[z * flat + i for i in range(flat)] for z in range(n0)]
    return lax.psum_scatter(
        partial, "seq", scatter_dimension=0, tiled=True, axis_index_groups=groups
    )


def scatter_plane_near(grid, partial):
    n0, n1, n2 = grid.sizes
    if (n1, n2) != (2, 2) or n0 % 2:
        return scatter_plane(grid, partial)
    width = partial.shape[1]
    blocks = partial.reshape(4, 2, -1, width)
    me = grid.coord[1] * 2 + grid.coord[2]
    own, by_x, by_y, across = [
        lax.dynamic_index_in_dim(blocks, lax.bitwise_xor(me, k), 0, False) for k in (0, 1, 2, 3)
    ]

    def plus(*terms):
        return sum(t.astype(F32) for t in terms).astype(BF)

    through_y, through_x = grid.shift(across[0], 1), grid.shift(across[1], 2)
    from_x = (grid.shift(plus(by_x[0], through_y), 2), grid.shift(by_x[1], 2))
    from_y = (grid.shift(by_y[0], 1), grid.shift(plus(by_y[1], through_x), 1))
    return jnp.concatenate([plus(own[j], from_x[j], from_y[j]) for j in (0, 1)], axis=0)


def plane_major(grid, values):
    n0, n1, n2 = grid.sizes
    width = values.shape[1]
    rows = width // grid.count
    flat = n1 * n2
    to = lax.broadcasted_iota(jnp.int32, (width, width), 0)
    of = lax.broadcasted_iota(jnp.int32, (width, width), 1)
    plane, z, row = to // (n0 * rows), (to // rows) % n0, to % rows
    pick = ((z * flat + plane) * rows + row == of).astype(BF)
    return rows_rows(pick, values).astype(BF)


def swap_mp(value):
    size = lax.axis_size("mp")
    return lax.ppermute(value, "mp", [(i, (i + 1) % size) for i in range(size)])


def mp_sum(value):
    low = value.astype(BF)
    return low.astype(F32) + swap_mp(low).astype(F32)


def mp_sum_exact(value):
    return value + swap_mp(value)


def seq_sum(value):
    count = lax.axis_size("seq")
    by = 1
    while by < count:
        value = value + lax.ppermute(value, "seq", [(i, i ^ by) for i in range(count)])
        by *= 2
    return value


def spread_small(grid, value):
    for dim in (2, 1, 0):
        n = grid.sizes[dim]
        me = grid.coord[dim]
        got = jnp.stack([value if k == 0 else grid.shift(value, dim, k) for k in range(n)])
        value = jnp.stack([lax.dynamic_index_in_dim(got, (me - j) % n, 0, False) for j in range(n)])
    return value


def scan_states(grid, table, state, reverse, event=None):
    heads = table.shape[-1]
    total = state.reshape(heads, state.shape[0] // heads, state.shape[1])
    enter = jnp.zeros_like(total)
    passed = jnp.ones((heads,), F32)
    levels = [d for d in (2, 1, 0) if grid.sizes[d] > 1]
    crossed = total
    for dim in levels:
        n = grid.sizes[dim]
        me = grid.coord[dim]
        group = table
        for slow in range(dim):
            group = lax.dynamic_index_in_dim(group, grid.coord[slow], 0, False)
        for _ in range(dim + 1, 3):
            group = jnp.prod(group, axis=1)
        index = lax.broadcasted_iota(jnp.int32, (n, 1), 0)

        def product(kept):
            return jnp.prod(jnp.where(kept, group, 1.0), axis=0)

        if event is not None and dim == levels[-1]:
            total = follow(total, event)
        low = total.astype(BF)
        if dim == levels[-1]:
            crossed = (crossed, low)
        summed = None
        for k in range(n):
            other = (me - k) % n
            ahead = (index < other) if reverse else (index > other)
            before = (index > me) if reverse else (index < me)
            got = total if k == 0 else grid.shift(low, dim, k).astype(F32)
            if k > 0:
                valid = (other > me) if reverse else (other < me)
                weight = jnp.where(valid, product(ahead & before) * passed, 0.0)
                enter = enter + weight[:, None, None] * got
            if dim != levels[-1]:
                term = product(ahead)[:, None, None] * got
                summed = term if summed is None else summed + term
        passed = passed * product((index > me) if reverse else (index < me))
        if dim != levels[-1]:
            crossed = total = summed
    return enter.reshape(state.shape), crossed


VMEM_ROOM = 60 * 2**20
SIDE = 128


def dims(a, b, exact=None):
    return functools.partial(
        lax.dot_general,
        dimension_numbers=(((a,), (b,)), ((), ())),
        precision=exact,
        preferred_element_type=F32,
    )


rows_cols = dims(1, 0)
rows_rows = dims(1, 1)
cols_cols = dims(0, 0)
exact_rc = dims(1, 0, PRECISE)
exact_rr = dims(1, 1, PRECISE)
exact_cc = dims(0, 0, PRECISE)


def call(body, name, shapes, flops, scratch=(), grid=None, in_specs=None, out_specs=None, moved=0):
    kw = {}
    if grid is not None:
        kw = dict(grid=grid, in_specs=in_specs, out_specs=out_specs)
    return pl.pallas_call(
        body,
        out_shape=shapes,
        scratch_shapes=list(scratch),
        name=name,
        compiler_params=pltpu.CompilerParams(vmem_limit_bytes=VMEM_ROOM),
        cost_estimate=pl.CostEstimate(flops=flops, bytes_accessed=moved, transcendentals=0),
        **kw,
    )


def half_lanes(n):
    return lax.broadcasted_iota(jnp.int32, (n, SIDE), 1) < LHD


def two_heads(values, low_half):
    none = jnp.zeros_like(values)
    return jnp.concatenate(
        [jnp.where(low_half, values, none), jnp.where(low_half, none, values)], axis=0
    )


def own_patch(n):
    row = lax.broadcasted_iota(jnp.int32, (n, n), 0)
    col = lax.broadcasted_iota(jnp.int32, (n, n), 1)
    return lax.div(row, PATCH) == lax.div(col, PATCH)


def gathered(values, mine):
    n = values.shape[0]
    kept = jnp.where(mine, values, 0.0).reshape(n // PATCH, PATCH, n)
    return jnp.sum(kept, axis=0)


def widened(values, mine):
    n = mine.shape[0]
    return jnp.where(mine, jnp.concatenate([values] * (n // PATCH), axis=0), 0.0).astype(BF)


def soft_block(scores, mine):
    n = scores.shape[0]
    key = lax.broadcasted_iota(jnp.int32, (PATCH, n), 0)
    query = lax.rem(lax.broadcasted_iota(jnp.int32, (PATCH, n), 1), PATCH)
    block = jnp.where(key <= query, gathered(scores, mine) * (LHD ** (-0.5)), -BIG)
    weights = jnp.exp(block - jnp.max(block, axis=0, keepdims=True))
    return weights / jnp.sum(weights, axis=0, keepdims=True)


def attend_body(width, qkv, out):
    n = qkv.shape[0]
    mine = own_patch(n)
    low_half = half_lanes(n)
    for p in range(width // SIDE):
        at = [slice(j * width + p * SIDE, j * width + (p + 1) * SIDE) for j in range(3)]
        q, k, v = qkv[:, at[0]], qkv[:, at[1]], qkv[:, at[2]]
        scores = rows_rows(two_heads(k, low_half), q)
        soft = [widened(soft_block(scores[j * n : (j + 1) * n], mine), mine) for j in range(2)]
        both = cols_cols(jnp.concatenate(soft, axis=0), two_heads(v, low_half))
        out[:, at[0]] = both.astype(BF)


def attend(qkv):
    rows, three = qkv.shape
    width = three // 3
    return call(
        functools.partial(attend_body, width),
        "attend",
        jax.ShapeDtypeStruct((rows, width), BF),
        rows * SIDE * width * 8,
        grid=(rows // SIDE,),
        in_specs=[pl.BlockSpec((SIDE, three), lambda i: (i, 0))],
        out_specs=pl.BlockSpec((SIDE, width), lambda i: (i, 0)),
        moved=rows * width * 8,
    )(qkv)


def attend_back_body(width, qkv, grad, out):
    n = qkv.shape[0]
    mine = own_patch(n)
    low_half = half_lanes(n)
    scale = LHD ** (-0.5)
    for p in range(width // SIDE):
        at = [slice(j * width + p * SIDE, j * width + (p + 1) * SIDE) for j in range(3)]
        q, k, v = qkv[:, at[0]], qkv[:, at[1]], qkv[:, at[2]]
        g = grad[:, at[0]]
        k_two = two_heads(k, low_half)
        scores = rows_rows(k_two, q)
        probs = rows_rows(two_heads(v, low_half), g)
        soft_wide, back_wide = [], []
        for j in range(2):
            rows = slice(j * n, (j + 1) * n)
            soft = soft_block(scores[rows], mine)
            prob = gathered(probs[rows], mine)
            back = soft * (prob - jnp.sum(soft * prob, axis=0, keepdims=True))
            soft_wide.append(widened(soft, mine))
            back_wide.append(widened(back, mine))
        q_grad = cols_cols(jnp.concatenate(back_wide, axis=0), k_two)
        k_grad = rows_cols(jnp.concatenate(back_wide, axis=1), two_heads(q, low_half))
        v_grad = rows_cols(jnp.concatenate(soft_wide, axis=1), two_heads(g, low_half))
        out[:, at[0]] = (q_grad * scale).astype(BF)
        out[:, at[1]] = (k_grad * scale).astype(BF)
        out[:, at[2]] = v_grad.astype(BF)


def attend_back(qkv, grad):
    rows, three = qkv.shape
    width = three // 3
    return call(
        functools.partial(attend_back_body, width),
        "attend_back",
        jax.ShapeDtypeStruct((rows, three), BF),
        rows * SIDE * width * 20,
        grid=(rows // SIDE,),
        in_specs=[
            pl.BlockSpec((SIDE, three), lambda i: (i, 0)),
            pl.BlockSpec((SIDE, width), lambda i: (i, 0)),
        ],
        out_specs=pl.BlockSpec((SIDE, three), lambda i: (i, 0)),
        moved=rows * width * 14,
    )(qkv, grad)


def middle_body(step, normed, grad, w_down, w_pair, hidden, pair):
    x = normed[...]
    gate = rows_cols(x, w_pair[:, :step])
    up = rows_cols(x, w_pair[:, step:])
    back = rows_cols(grad[...], w_down[...])
    sig = 1.0 / (1.0 + jnp.exp(-gate))
    act = gate * sig
    hidden[...] = (act * up).astype(BF)
    pair[:, step:] = (back * act).astype(BF)
    pair[:, :step] = (back * up * sig * (1.0 + gate * (1.0 - sig))).astype(BF)


def middle(normed, grad, w_all, ff, step):
    rows, width = normed.shape
    return call(
        functools.partial(middle_body, step),
        "middle",
        (jax.ShapeDtypeStruct((rows, ff), BF), jax.ShapeDtypeStruct((rows, 2 * ff), BF)),
        rows * width * ff * 6,
        grid=(ff // step,),
        in_specs=[
            pl.BlockSpec((rows, width), lambda i: (0, 0)),
            pl.BlockSpec((rows, width), lambda i: (0, 0)),
            pl.BlockSpec((width, step), lambda i: (0, i)),
            pl.BlockSpec((width, 2 * step), lambda i: (0, i + ff // (2 * step))),
        ],
        out_specs=(
            pl.BlockSpec((rows, step), lambda i: (0, i)),
            pl.BlockSpec((rows, 2 * step), lambda i: (0, i)),
        ),
        moved=rows * width * 4 + width * ff * 6 + rows * ff * 6,
    )(normed, grad, w_all, w_all)


def products_body(starts, *refs):
    count = len(starts) - 1
    out = refs[2 * count]
    for j in range(count):

        @pl.when((pl.program_id(0) >= starts[j]) & (pl.program_id(0) < starts[j + 1]))
        def _(j=j):
            out[...] = rows_cols(refs[2 * j][...], refs[2 * j + 1][...]).astype(out.dtype)


def products(pairs, step):
    starts = [0]
    in_specs, args, flops, moved = [], [], 0, 0
    for left, right in pairs:
        first, runs = starts[-1], right.shape[1] // step
        starts.append(first + runs)
        in_specs.append(pl.BlockSpec(left.shape, lambda i: (0, 0)))

        def column(i, first=first, runs=runs):
            return (0, jnp.clip(i - first, 0, runs - 1))

        in_specs.append(pl.BlockSpec((right.shape[0], step), column))
        args += [left, right]
        flops += 2 * left.shape[0] * right.shape[0] * right.shape[1]
        moved += 2 * (left.size + right.size)
    m = pairs[0][0].shape[0]
    return call(
        functools.partial(products_body, tuple(starts)),
        "products",
        jax.ShapeDtypeStruct((m, starts[-1] * step), BF),
        flops,
        grid=(starts[-1],),
        in_specs=in_specs,
        out_specs=pl.BlockSpec((m, step), lambda i: (0, i)),
        moved=moved + 2 * m * starts[-1] * step,
    )(*args)


def softplus_fn(values):
    return jnp.log1p(jnp.exp(-jnp.abs(values))) + jnp.maximum(values, 0.0)


def lower_ones(n):
    row = lax.broadcasted_iota(jnp.int32, (n, n), 0)
    col = lax.broadcasted_iota(jnp.int32, (n, n), 1)
    return row >= col


def taps_fill(rim, mixed, buf, taps):
    buf[0:8, :] = rim[...].astype(F32)
    buf[8 : 8 + mixed.shape[0], :] = mixed[...].astype(F32)


def conv_here(buf, k_x, k_bc, info, n, taps):
    wide = jnp.concatenate([k_x[...], k_bc[...]], axis=1)
    total = None
    for k in range(taps):
        at = 9 - taps + k
        term = buf[at : at + n, :] * wide[k : k + 1, :] * info[:, k : k + 1]
        total = term if total is None else total + term
    return total


def decays(raw, small, n):
    base = raw[...] + small[0:1, :]
    step = softplus_fn(base)
    rate = jnp.exp(small[1:2, :])
    log_decay = -step * rate
    tri = lower_ones(n).astype(F32)
    cum = exact_rc(tri, log_decay)
    return base, step, rate, log_decay, tri, cum


def mix_body(taps, inner, rim, mixed, raw, small, skip, k_x, k_bc, info, seg, y_out, c_out, din_out, state_out, buf):
    n = mixed.shape[0]
    taps_fill(rim, mixed, buf, taps)
    pre = conv_here(buf, k_x, k_bc, info, n, taps)
    act = pre / (1.0 + jnp.exp(-pre))
    b = act[:, inner : inner + SIDE]
    c = act[:, inner + SIDE :]
    _, step, _, _, _, cum = decays(raw, small, n)
    cum_t, step_t = cum.T, step.T
    live = lower_ones(n) & (info[:, 6:7] == seg[0:1, :])
    both = exact_rr(c, b)
    din_out[...] = info[:, 4:5] * jnp.exp(cum)
    tail = jnp.exp(jnp.where(info[:, 5:6] > 0.0, cum[n - 1 : n, :] - cum, -BIG)) * step
    low_half = half_lanes(n)
    c_out[...] = c
    for p in range(inner // SIDE):
        at = slice(p * SIDE, (p + 1) * SIDE)
        x = act[:, at]
        y = skip[0:1, at] * x
        for j, mine in enumerate((low_half, ~low_half)):
            h = 2 * p + j
            gaps = jnp.exp(jnp.where(live, cum[:, h : h + 1] - cum_t[h : h + 1, :], -BIG))
            mix = both * gaps * step_t[h : h + 1, :]
            y = y + exact_rc(mix, jnp.where(mine, x, 0.0))
        y_out[:, at] = y
        weighted = x * jnp.where(low_half, tail[:, 2 * p : 2 * p + 1], tail[:, 2 * p + 1 : 2 * p + 2])
        state_out[at, :] = exact_cc(weighted, b)


def mix(rim, mixed, raw, small, skip, k_x, k_bc, info, seg):
    n, wide = mixed.shape
    taps, inner = k_x.shape
    return call(
        functools.partial(mix_body, taps, inner),
        "mix",
        (
            jax.ShapeDtypeStruct((n, inner), F32),
            jax.ShapeDtypeStruct((n, SIDE), F32),
            jax.ShapeDtypeStruct((n, SIDE), F32),
            jax.ShapeDtypeStruct((inner, SIDE), F32),
        ),
        n * n * inner * 24,
        scratch=(pltpu.VMEM((n + 8, wide), F32),),
        moved=n * inner * 20,
    )(rim, mixed, raw, small, skip, k_x, k_bc, info, seg)


def pair_cols(values, p, low_half):
    return jnp.where(low_half, values[:, 2 * p : 2 * p + 1], values[:, 2 * p + 1 : 2 * p + 2])


def finish_body(inner, y_part, c, din, state, z, y_out, gated_out, square):
    n = y_part.shape[0]
    low_half = half_lanes(n)
    total = None
    for p in range(inner // SIDE):
        at = slice(p * SIDE, (p + 1) * SIDE)
        y = y_part[:, at] + pair_cols(din, p, low_half) * exact_rr(c[...], state[at, :])
        gate = z[:, at]
        gated = y * (gate / (1.0 + jnp.exp(-gate)))
        y_out[:, at] = y
        gated_out[:, at] = gated
        term = gated * gated
        total = term if total is None else total + term
    square[...] = jnp.broadcast_to(jnp.sum(total, axis=1, keepdims=True), square.shape)


def finish(y_part, c, din, state, z):
    n, inner = y_part.shape
    return call(
        functools.partial(finish_body, inner),
        "finish",
        (
            jax.ShapeDtypeStruct((n, inner), F32),
            jax.ShapeDtypeStruct((n, inner), F32),
            jax.ShapeDtypeStruct((n, SIDE), F32),
        ),
        n * SIDE * inner * 12,
        moved=n * inner * 20,
    )(y_part, c, din, state, z)


def unfinish_body(inner, y_norm_grad, gated, y_full, z, gain, stats, din, c, y_grad, z_grad, state_grad):
    n = gated.shape[0]
    low_half = half_lanes(n)
    for p in range(inner // SIDE):
        at = slice(p * SIDE, (p + 1) * SIDE)
        back = stats[:, 0:1] * (y_norm_grad[:, at] * gain[0:1, at]) - gated[:, at] * stats[:, 1:2]
        gate = z[:, at]
        sig = 1.0 / (1.0 + jnp.exp(-gate))
        y_back = back * gate * sig
        y_grad[:, at] = y_back
        z_grad[:, at] = (back * y_full[:, at] * sig * (1.0 + gate * (1.0 - sig))).astype(BF)
        state_grad[at, :] = exact_cc(y_back * pair_cols(din, p, low_half), c[...])


def unfinish(y_norm_grad, gated, y_full, z, gain, stats, din, c):
    n, inner = gated.shape
    return call(
        functools.partial(unfinish_body, inner),
        "unfinish",
        (
            jax.ShapeDtypeStruct((n, inner), F32),
            jax.ShapeDtypeStruct((n, inner), BF),
            jax.ShapeDtypeStruct((inner, SIDE), F32),
        ),
        n * SIDE * inner * 12,
        moved=n * inner * 24,
    )(y_norm_grad, gated, y_full, z, gain, stats, din, c)


def unmix_body(
    taps, inner, rim, mixed, raw, small, skip, k_x, k_bc, info, seg, y_grad, state_in, state_back,
    ext_out, raw_out, taps_out, heads_out, skip_out, buf, d_buf, d_act, cols, sums, steps,
):
    n = mixed.shape[0]
    taps_fill(rim, mixed, buf, taps)
    pre = conv_here(buf, k_x, k_bc, info, n, taps)
    sig_pre = 1.0 / (1.0 + jnp.exp(-pre))
    act = pre * sig_pre
    b = act[:, inner : inner + SIDE]
    c = act[:, inner + SIDE :]
    base, step, rate, log_decay, tri, cum = decays(raw, small, n)
    cum_t, step_t = cum.T, step.T
    live = lower_ones(n) & (info[:, 6:7] == seg[0:1, :])
    both = exact_rr(c, b)
    din = info[:, 4:5] * jnp.exp(cum)
    tail = jnp.exp(jnp.where(info[:, 5:6] > 0.0, cum[n - 1 : n, :] - cum, -BIG))
    low_half = half_lanes(n)
    cols[...] = jnp.zeros_like(cols)
    sums[...] = jnp.zeros_like(sums)
    steps[...] = jnp.zeros_like(steps)
    both_grad = jnp.zeros((n, n), F32)
    b_grad = jnp.zeros((n, SIDE), F32)
    c_grad = jnp.zeros((n, SIDE), F32)
    lane = lax.broadcasted_iota(jnp.int32, (1, SIDE), 1)
    total_grad = jnp.zeros((1, SIDE), F32)
    tail_grad = jnp.zeros((n, SIDE), F32)
    for p in range(inner // SIDE):
        at = slice(p * SIDE, (p + 1) * SIDE)
        x = act[:, at]
        dy = y_grad[:, at]
        s_in = state_in[at, :]
        s_back = state_back[at, :]
        out_b = exact_rr(b, s_back)
        weight = pair_cols(tail, p, low_half) * pair_cols(step, p, low_half)
        dx = skip[0:1, at] * dy + weight * out_b
        b_grad = b_grad + exact_rc(x * weight, s_back)
        dy_in = pair_cols(din, p, low_half) * dy
        in_c = exact_rr(c, s_in)
        c_grad = c_grad + exact_rc(dy_in, s_in)
        skip_out[0:1, at] = jnp.sum(dy * x, axis=0, keepdims=True)
        held = jnp.sum(s_in * s_back, axis=1, keepdims=True)
        for j, mine in enumerate((low_half, ~low_half)):
            h = 2 * p + j
            dy_mine = jnp.where(mine, dy, 0.0)
            gaps = jnp.exp(jnp.where(live, cum[:, h : h + 1] - cum_t[h : h + 1, :], -BIG))
            step_row = step_t[h : h + 1, :]
            back = exact_rr(dy_mine, x) * gaps
            both_grad = both_grad + back * step_row
            back = back * both
            each = back * step_row
            dx = dx + exact_cc(both * gaps * step_row, dy_mine)
            steps[h : h + 1, :] = jnp.sum(back, axis=0, keepdims=True)
            sums[h : h + 1, :] = -jnp.sum(each, axis=0, keepdims=True)
            from_in = jnp.sum(jnp.where(mine, dy_in * in_c, 0.0), axis=1, keepdims=True)
            cols[:, h : h + 1] = jnp.sum(each, axis=1, keepdims=True) + from_in
            from_tail = jnp.sum(jnp.where(mine, x * out_b, 0.0), axis=1, keepdims=True)
            tail_grad = tail_grad + jnp.where(lane == h, from_tail, 0.0)
            here = jnp.sum(held[j * LHD : (j + 1) * LHD, :], axis=0, keepdims=True)
            total_grad = total_grad + jnp.where(lane == h, here, 0.0)
        d_act[:, at] = dx
    d_act[:, inner : inner + SIDE] = b_grad + exact_cc(both_grad, c)
    d_act[:, inner + SIDE :] = c_grad + exact_rc(both_grad, b)
    tail_back = tail_grad * tail
    row = lax.broadcasted_iota(jnp.int32, (n, SIDE), 0)
    moved = tail_back * step
    last = jnp.sum(moved, axis=0, keepdims=True) + total_grad * din[n - 1 : n, :]
    cum_grad = cols[...] + sums[...].T - moved + jnp.where(row == n - 1, last, 0.0)
    decay_grad = exact_cc(tri, cum_grad)
    step_grad = steps[...].T + tail_back - decay_grad * rate
    raw_grad = step_grad / (1.0 + jnp.exp(-base))
    raw_out[...] = raw_grad
    heads_out[0:1, :] = jnp.sum(raw_grad, axis=0, keepdims=True)
    heads_out[1:2, :] = jnp.sum(decay_grad * log_decay, axis=0, keepdims=True)
    heads_out[2:8, :] = jnp.zeros((6, SIDE), F32)
    d_pre = d_act[...] * (sig_pre * (1.0 + pre * (1.0 - sig_pre)))
    d_buf[...] = jnp.zeros_like(d_buf)
    wide = jnp.concatenate([k_x[...], k_bc[...]], axis=1)
    for k in range(taps):
        at = 9 - taps + k
        masked = d_pre * info[:, k : k + 1]
        d_buf[at : at + n, :] = d_buf[at : at + n, :] + masked * wide[k : k + 1, :]
        taps_out[k : k + 1, :] = jnp.sum(masked * buf[at : at + n, :], axis=0, keepdims=True)
    ext_out[...] = d_buf[...]


def unmix(rim, mixed, raw, small, skip, k_x, k_bc, info, seg, y_grad, state_in, state_back):
    n, wide = mixed.shape
    taps, inner = k_x.shape
    return call(
        functools.partial(unmix_body, taps, inner),
        "unmix",
        (
            jax.ShapeDtypeStruct((n + 8, wide), F32),
            jax.ShapeDtypeStruct((n, SIDE), F32),
            jax.ShapeDtypeStruct((taps, wide), F32),
            jax.ShapeDtypeStruct((8, SIDE), F32),
            jax.ShapeDtypeStruct((1, inner), F32),
        ),
        n * n * inner * 96,
        scratch=(
            pltpu.VMEM((n + 8, wide), F32),
            pltpu.VMEM((n + 8, wide), F32),
            pltpu.VMEM((n, wide), F32),
            pltpu.VMEM((n, SIDE), F32),
            pltpu.VMEM((SIDE, n), F32),
            pltpu.VMEM((SIDE, n), F32),
        ),
        moved=n * inner * 30,
    )(rim, mixed, raw, small, skip, k_x, k_bc, info, seg, y_grad, state_in, state_back)


def bf_dot(left, right):
    return rows_cols(left, right)


def dot_t(left, right):
    return rows_rows(left, right)


def grad_dot(left, right):
    return cols_cols(left, right)


def rms_rows(values):
    return lax.rsqrt(jnp.mean(values * values, axis=-1, keepdims=True) + EPS)


def norm_back(grad_in, values, rstd_rows, gain_row):
    normed_rows = values * rstd_rows
    gain_grad = jnp.sum(grad_in * normed_rows, axis=0)
    scaled = grad_in * gain_row[None, :]
    input_grad = rstd_rows * (
        scaled - normed_rows * jnp.mean(scaled * normed_rows, axis=-1, keepdims=True)
    )
    return (input_grad, gain_grad)


def local(
    seq_count,
    bytes_in,
    out_grad,
    seq_ids,
    norm_gain,
    w_z,
    w_x,
    w_bc,
    w_dt,
    w_out,
    attn_gain,
    w_q,
    w_k,
    w_v,
    w_o,
    mlp_gain,
    w_gate,
    w_up,
    w_down,
    dt_bias,
    a_log,
    d_skip,
    conv_x,
    conv_bc,
    inner_gain,
):
    grid = Grid(seq_count)
    rows, ff = w_gate.shape
    inner = w_x.shape[1]
    bc_width = w_bc.shape[1]
    heads = w_dt.shape[1]
    attn_width = w_q.shape[1]
    step = min(256, ff)
    byte_rows, model_width = bytes_in.shape
    patch_rows = byte_rows // PATCH
    taps = conv_x.shape[0]
    inner_full = inner * lax.axis_size("mp")

    first = jnp.concatenate(
        [
            w_x.astype(BF),
            w_bc.astype(BF),
            w_dt.astype(BF),
            norm_gain.astype(BF)[:, None],
            attn_gain.astype(BF)[:, None],
            mlp_gain.astype(BF)[:, None],
            jnp.zeros((rows, SIDE - heads - 3), BF),
        ],
        axis=1,
    )
    first_column = gather_column(grid, first)
    first_all = gather_plane(grid, first_column)
    second = jnp.concatenate(
        [w.astype(BF) for w in (w_z, w_out.T, w_q, w_k, w_v, w_o.T)], axis=1
    )
    second = follow(second, first_column)
    pair = jnp.stack(
        [w.astype(BF).reshape(rows, ff // step, step) for w in (w_gate, w_up)], axis=2
    ).reshape(rows, 2 * ff)
    mlp = jnp.concatenate([w_down.T.astype(BF), pair], axis=1)

    tail_all = first_all[:, inner + bc_width :]
    gains = tail_all[:, heads : heads + 3].astype(F32).T
    norm_row, attn_row, mlp_row = gains[0], gains[1], gains[2]
    x_float = bytes_in.astype(F32)
    patch_in = jnp.mean(x_float.reshape(patch_rows, PATCH, model_width), axis=1)
    rstd_patch = rms_rows(patch_in)
    h_norm = (patch_in * rstd_patch * norm_row[None, :]).astype(BF)
    into = bf_dot(h_norm, first_all)
    mixed = into[:, : inner + bc_width].astype(BF)
    raw = into[:, inner + bc_width :]
    second_column = gather_column(grid, second, mixed)
    second_all = gather_plane_off(grid, second_column).reshape(model_width, -1)
    z_all, out_all = second_all[:, :inner], second_all[:, inner : 2 * inner]
    third_all = second_all[:, 2 * inner :]
    qkv_all, wo_all = third_all[:, : 3 * attn_width], third_all[:, 3 * attn_width :]
    rim = lax.ppermute(
        mixed[patch_rows - (taps - 1) :], "seq", [(i, i + 1) for i in range(seq_count - 1)]
    )
    rim = jnp.pad(rim, ((8 - (taps - 1), 0), (0, 0)))
    first_row = lax.axis_index("seq") * patch_rows
    ids_padded = jnp.concatenate([jnp.full((taps - 1,), -1, jnp.int32), seq_ids])
    ids_ext = lax.dynamic_slice_in_dim(ids_padded, first_row, patch_rows + taps - 1)
    ids = ids_ext[taps - 1 :]
    columns = [ids_ext[k : k + patch_rows] == ids for k in range(taps)]
    columns += [ids == ids_ext[taps - 2], ids == ids[patch_rows - 1], ids]
    info = jnp.stack([c.astype(F32) for c in columns], axis=1)
    info = jnp.pad(info, ((0, 0), (0, SIDE - info.shape[1])))
    seg = jnp.broadcast_to(ids.astype(F32)[None, :], (8, patch_rows))
    small = jnp.pad(jnp.stack([dt_bias, a_log]), ((0, 6), (0, SIDE - heads)))
    skip = jnp.repeat(d_skip, inner // heads)[None, :]
    whole = jnp.sum(softplus_fn(raw[:, :heads] + dt_bias), axis=0) * -jnp.exp(a_log)
    table = spread_small(grid, info[patch_rows - 1, taps] * jnp.exp(whole))
    known = (rim, mixed, raw, small, skip, conv_x, conv_bc, info, seg)
    y_part, c_rows, decay_in, state_own = mix(*known)
    state_in, (crossed, _) = scan_states(grid, table, state_own, False)
    mlp_column = gather_column(grid, follow(mlp, first_all, second_column), crossed)
    mlp_all = gather_plane_off(grid, follow(mlp_column, second_all)).reshape(model_width, -1)
    down_all, pair_all = mlp_all[:, :ff], mlp_all[:, ff:]
    gate_z = bf_dot(h_norm, z_all)
    y_full, gated, square = finish(y_part, c_rows, decay_in, state_in, gate_z)
    square_sum = mp_sum_exact(square[:, 0])
    rstd_inner = lax.rsqrt(square_sum / inner_full + EPS)[:, None]
    y_norm = (gated * rstd_inner * inner_gain[None, :]).astype(BF)
    mixer_out = mp_sum(dot_t(y_norm, out_all))
    patch_out = patch_in + mixer_out

    rows_in = x_float + jnp.repeat(patch_out, PATCH, axis=0)
    rstd_attn = rms_rows(rows_in)
    normed = (rows_in * rstd_attn * attn_row[None, :]).astype(BF)
    qkv = bf_dot(normed, qkv_all).astype(BF)
    attended = attend(qkv)
    after_attn = rows_in + mp_sum(dot_t(attended, wo_all))
    rstd_mlp = rms_rows(after_attn)
    normed_mlp = (after_attn * rstd_mlp * mlp_row[None, :]).astype(BF)
    hidden, pair_grad = middle(normed_mlp, out_grad, mlp_all, ff, step)
    block_out = after_attn + mp_sum(dot_t(hidden, down_all))

    mlp_part = products(
        (
            (plane_major(grid, normed_mlp), pair_grad),
            (plane_major(grid, out_grad), hidden),
        ),
        2 * step,
    )
    mlp_plane = scatter_plane(grid, mlp_part)
    pair_grad = follow(pair_grad, mlp_part)
    mlp_norm_grad = mp_sum(dot_t(pair_grad, pair_all))
    mlp_in_grad, mlp_gain_grad = norm_back(mlp_norm_grad, after_attn, rstd_mlp, mlp_row)
    after_grad = out_grad.astype(F32) + mlp_in_grad
    after_low = after_grad.astype(BF)
    attended_grad = bf_dot(after_low, wo_all).astype(BF)
    qkv_grad = attend_back(qkv, attended_grad)
    attn_norm_grad = mp_sum(dot_t(qkv_grad, qkv_all))
    attn_in_grad, attn_gain_grad = norm_back(attn_norm_grad, rows_in, rstd_attn, attn_row)
    rows_grad = after_grad + attn_in_grad
    patch_grad = jnp.sum(rows_grad.reshape(patch_rows, PATCH, model_width), axis=1)
    patch_low = patch_grad.astype(BF)
    y_norm_grad = bf_dot(patch_low, out_all)
    shared = y_norm_grad * gated
    inner_gain_grad = jnp.sum(shared * rstd_inner, axis=0)
    cross_sum = mp_sum_exact(jnp.sum(shared * inner_gain[None, :], axis=-1))[:, None]
    stats = jnp.concatenate([rstd_inner, rstd_inner**3 * (cross_sum / inner_full)], axis=1)
    stats = jnp.pad(stats, ((0, 0), (0, SIDE - 2)))
    y_grad, z_low, state_in_grad = unfinish(
        y_norm_grad, gated, y_full, gate_z, inner_gain[None, :], stats, decay_in, c_rows
    )
    h_norm_t = plane_major(grid, h_norm)
    rest_part = products(
        (
            (plane_major(grid, normed), qkv_grad),
            (plane_major(grid, after_low), attended),
            (h_norm_t, z_low),
            (plane_major(grid, patch_low), y_norm),
        ),
        attn_width,
    )
    state_in_grad = follow(state_in_grad, rest_part)
    state_grad, (crossed, sent) = scan_states(grid, table, state_in_grad, True, mlp_plane)
    rest_plane = scatter_plane(grid, follow(rest_part, mlp_plane, crossed))
    mlp_sums = [
        scatter_column(grid, follow(mlp_plane[:, i : i + ff], sent)) for i in (0, ff, 2 * ff)
    ]
    ext_grad, raw_grad, taps_grad, heads_grad, skip_grad = unmix(
        *known, y_grad, state_in, state_grad
    )
    bc_total = mp_sum(ext_grad[:, inner:])
    conv_bc_grad = mp_sum_exact(taps_grad[:, inner:])
    ext_full = jnp.concatenate([ext_grad[:, :inner], bc_total], axis=1)
    rim_back = lax.ppermute(
        ext_full[8 - (taps - 1) : 8], "seq", [(i + 1, i) for i in range(seq_count - 1)]
    )
    mixed_low = (
        ext_full[8:] + jnp.pad(rim_back, ((patch_rows - (taps - 1), 0), (0, 0)))
    ).astype(BF)
    first_grad = jnp.concatenate([mixed_low, raw_grad.astype(BF)], axis=1)
    first_grad = follow(first_grad, mlp_sums[0])
    first_part = bf_dot(h_norm_t, first_grad).astype(BF)
    first_grad = follow(first_grad, first_part)
    first_plane = scatter_plane(grid, follow(first_part, rest_plane))
    lane = lax.broadcasted_iota(jnp.int32, (1, first_grad.shape[1]), 1)
    twice = (lane >= inner) & (lane < inner + bc_width) & (lax.axis_index("mp") > 0)
    cut = 4 * attn_width
    rest_sums = [
        scatter_column(grid, part) for part in (rest_plane[:, :cut], rest_plane[:, cut:])
    ]
    first_grad = follow(first_grad, mlp_sums[1])
    own_grad = jnp.where(twice, jnp.zeros_like(first_grad), first_grad)
    h_grad = mp_sum(dot_t(own_grad, first_all) + dot_t(z_low, z_all))
    patch_in_grad, norm_gain_grad = norm_back(h_grad, patch_in, rstd_patch, norm_row)
    patch_total = follow(patch_grad + patch_in_grad, rest_sums[1])
    bytes_grad = rows_grad + jnp.repeat(patch_total / PATCH, PATCH, axis=0)

    pair_sum = jnp.concatenate(mlp_sums[:2], axis=1).reshape(rows, ff // step, 2, step)
    w_gate_grad = pair_sum[:, :, 0].reshape(rows, ff)
    w_up_grad = pair_sum[:, :, 1].reshape(rows, ff)
    w_down_grad = mlp_sums[2].T
    first_sum = scatter_column(grid, first_plane)
    w_qkv_grad, w_o_grad = (
        rest_sums[0][:, : 3 * attn_width],
        rest_sums[0][:, 3 * attn_width :].T,
    )
    w_z_grad, w_out_grad = rest_sums[1][:, :inner], rest_sums[1][:, inner:].T

    pieces = (
        heads_grad[:2],
        skip_grad,
        taps_grad[:, :inner],
        conv_bc_grad,
        inner_gain_grad,
        norm_gain_grad,
        attn_gain_grad,
        mlp_gain_grad,
    )
    flat = seq_sum(jnp.concatenate([p.reshape(-1, SIDE) for p in pieces], axis=0))
    parts, start = [], 0
    for p in pieces:
        stop = start + p.size // SIDE
        parts.append(flat[start:stop].reshape(p.shape))
        start = stop
    mine = lax.axis_index("seq") * rows
    gain_parts = [lax.dynamic_slice_in_dim(g, mine, rows) for g in parts[5:]]
    return (
        block_out,
        bytes_grad,
        gain_parts[0],
        w_z_grad,
        first_sum[:, :inner],
        first_sum[:, inner : inner + bc_width],
        first_sum[:, inner + bc_width : inner + bc_width + heads],
        w_out_grad,
        gain_parts[1],
        w_qkv_grad[:, :attn_width],
        w_qkv_grad[:, attn_width : 2 * attn_width],
        w_qkv_grad[:, 2 * attn_width :],
        w_o_grad,
        gain_parts[2],
        w_gate_grad,
        w_up_grad,
        w_down_grad,
        parts[0][0, :heads],
        parts[0][1, :heads],
        jnp.sum(parts[1].reshape(heads, inner // heads), axis=1),
        parts[2],
        parts[3],
        parts[4],
    )


def solution(mesh):
    rows, cols, both, rest = P("seq", None), P("seq", "mp"), P("mp", "seq"), P()
    vec, per = P("seq"), P("mp")
    weights = (vec, cols, cols, rows, cols, both, vec, cols, cols, cols, both, vec, cols, cols, both)
    small = (per, per, per, P(None, "mp"), rest, per)
    in_specs = (rows, rows, rest) + weights + small
    out_specs = (rows, rows) + weights + small
    body = functools.partial(local, mesh.shape["seq"])
    return jax.shard_map(body, mesh=mesh, in_specs=in_specs, out_specs=out_specs, check_vma=False)
```

```python
import functools

import jax
import jax.numpy as jnp
from jax import lax
from jax.experimental import pallas as pl
from jax.experimental.pallas import tpu as pltpu
from jax.sharding import PartitionSpec as P

LHD = 64
PATCH = 8
EPS = 1e-05
BIG = 1e30
PRECISE = lax.Precision.HIGHEST
BF = jnp.bfloat16
F32 = jnp.float32


def factors(count):
    root = 1
    while (root * 2) ** 3 <= count:
        root *= 2
    rest = count // root
    middle = root if rest % root == 0 and rest // root >= root else 1
    return (rest // middle, middle, root)


class Grid:
    def __init__(self, count):
        self.count = count
        self.sizes = factors(count)
        self.place = lax.axis_index("seq")
        n0, n1, n2 = self.sizes
        self.coord = (self.place // (n1 * n2), (self.place // n2) % n1, self.place % n2)

    def pairs(self, dim, by):
        n0, n1, n2 = self.sizes
        out = []
        for i in range(self.count):
            c = [i // (n1 * n2), (i // n2) % n1, i % n2]
            c[dim] = (c[dim] + by) % self.sizes[dim]
            out.append((i, (c[0] * n1 + c[1]) * n2 + c[2]))
        return out

    def shift(self, value, dim, by=1):
        return lax.ppermute(value, "seq", self.pairs(dim, by))


def follow(value, *events):
    return lax.optimization_barrier((value,) + events)[0]


def spread(grid, block, dim, events=()):
    n = grid.sizes[dim]
    me = grid.coord[dim]
    got = [block] + [grid.shift(block, dim, k) for k in range(1, n)]
    if events:
        got = [got[0]] + [follow(g, *events) for g in got[1:]]
    if n == 1:
        return block[None]
    if n == 2:
        first = me == 0
        return jnp.stack([jnp.where(first, got[0], got[1]), jnp.where(first, got[1], got[0])])
    out = jnp.zeros((n,) + block.shape, block.dtype)
    for k, part in enumerate(got):
        out = lax.dynamic_update_index_in_dim(out, part, (me - k) % n, 0)
    return out


def gather_column(grid, block, *events):
    return spread(grid, block, 0, events)


def gather_plane_off(grid, column):
    n0, n1, n2 = grid.sizes
    flat = n1 * n2
    groups = [[z * flat + i for i in range(flat)] for z in range(n0)]
    return lax.all_gather(column, "seq", axis=1, tiled=False, axis_index_groups=groups)


def gather_plane(grid, column):
    n0, n1, n2 = grid.sizes
    _, rows, width = column.shape
    if (n1, n2) != (2, 2) or n0 % 2:
        block = spread(grid, spread(grid, column, 1), 2)
        block = jnp.transpose(block, (2, 1, 0, 3, 4))
        return block.reshape(grid.count * rows, width)
    half = n0 // 2
    parts = (column[:half], column[half:])
    by_x = [grid.shift(p, 2) for p in parts]
    by_y = [grid.shift(p, 1) for p in parts]
    across = [grid.shift(by_x[0], 1), grid.shift(by_y[1], 2)]
    own, by_x, by_y, across = [
        jnp.concatenate(p, axis=0) for p in (parts, by_x, by_y, across)
    ]
    me_y, me_x = grid.coord[1], grid.coord[2]
    tiles = []
    for y in range(2):
        row = []
        for x in range(2):
            same = jnp.where(me_x == x, own, by_x)
            other = jnp.where(me_x == x, by_y, across)
            row.append(jnp.where(me_y == y, same, other))
        tiles.append(jnp.stack(row, axis=1))
    return jnp.stack(tiles, axis=1).reshape(grid.count * rows, width)


def scatter_column(grid, total):
    n = grid.sizes[0]
    me = grid.coord[0]
    total = total.reshape(n, total.shape[0] // n, total.shape[1])
    summed = lax.dynamic_index_in_dim(total, me, 0, False).astype(F32)
    for k in range(1, n):
        block = lax.dynamic_index_in_dim(total, (me + k) % n, 0, False)
        summed = summed + grid.shift(block, 0, k).astype(F32)
    return summed


def scatter_plane(grid, partial):
    n0, n1, n2 = grid.sizes
    flat = n1 * n2
    groups = [[z * flat + i for i in range(flat)] for z in range(n0)]
    return lax.psum_scatter(
        partial, "seq", scatter_dimension=0, tiled=True, axis_index_groups=groups
    )


def scatter_plane_near(grid, partial):
    n0, n1, n2 = grid.sizes
    if (n1, n2) != (2, 2) or n0 % 2:
        return scatter_plane(grid, partial)
    width = partial.shape[1]
    blocks = partial.reshape(4, 2, -1, width)
    me = grid.coord[1] * 2 + grid.coord[2]
    own, by_x, by_y, across = [
        lax.dynamic_index_in_dim(blocks, lax.bitwise_xor(me, k), 0, False) for k in (0, 1, 2, 3)
    ]

    def plus(*terms):
        return sum(t.astype(F32) for t in terms).astype(BF)

    through_y, through_x = grid.shift(across[0], 1), grid.shift(across[1], 2)
    from_x = (grid.shift(plus(by_x[0], through_y), 2), grid.shift(by_x[1], 2))
    from_y = (grid.shift(by_y[0], 1), grid.shift(plus(by_y[1], through_x), 1))
    return jnp.concatenate([plus(own[j], from_x[j], from_y[j]) for j in (0, 1)], axis=0)


def plane_major(grid, values):
    n0, n1, n2 = grid.sizes
    width = values.shape[1]
    rows = width // grid.count
    flat = n1 * n2
    to = lax.broadcasted_iota(jnp.int32, (width, width), 0)
    of = lax.broadcasted_iota(jnp.int32, (width, width), 1)
    plane, z, row = to // (n0 * rows), (to // rows) % n0, to % rows
    pick = ((z * flat + plane) * rows + row == of).astype(BF)
    return rows_rows(pick, values).astype(BF)


def swap_mp(value):
    size = lax.axis_size("mp")
    return lax.ppermute(value, "mp", [(i, (i + 1) % size) for i in range(size)])


def mp_sum(value):
    low = value.astype(BF)
    return low.astype(F32) + swap_mp(low).astype(F32)


def mp_sum_exact(value):
    return value + swap_mp(value)


def seq_sum(value):
    count = lax.axis_size("seq")
    by = 1
    while by < count:
        value = value + lax.ppermute(value, "seq", [(i, i ^ by) for i in range(count)])
        by *= 2
    return value


def spread_small(grid, value):
    for dim in (2, 1, 0):
        n = grid.sizes[dim]
        me = grid.coord[dim]
        got = jnp.stack([value if k == 0 else grid.shift(value, dim, k) for k in range(n)])
        value = jnp.stack([lax.dynamic_index_in_dim(got, (me - j) % n, 0, False) for j in range(n)])
    return value


def scan_states(grid, table, state, reverse, event=None):
    heads = table.shape[-1]
    total = state.reshape(heads, state.shape[0] // heads, state.shape[1])
    enter = jnp.zeros_like(total)
    passed = jnp.ones((heads,), F32)
    levels = [d for d in (2, 1, 0) if grid.sizes[d] > 1]
    crossed = total
    for dim in levels:
        n = grid.sizes[dim]
        me = grid.coord[dim]
        group = table
        for slow in range(dim):
            group = lax.dynamic_index_in_dim(group, grid.coord[slow], 0, False)
        for _ in range(dim + 1, 3):
            group = jnp.prod(group, axis=1)
        index = lax.broadcasted_iota(jnp.int32, (n, 1), 0)

        def product(kept):
            return jnp.prod(jnp.where(kept, group, 1.0), axis=0)

        if event is not None and dim == levels[-1]:
            total = follow(total, event)
        low = total.astype(BF)
        if dim == levels[-1]:
            crossed = (crossed, low)
        summed = None
        for k in range(n):
            other = (me - k) % n
            ahead = (index < other) if reverse else (index > other)
            before = (index > me) if reverse else (index < me)
            got = total if k == 0 else grid.shift(low, dim, k).astype(F32)
            if k > 0:
                valid = (other > me) if reverse else (other < me)
                weight = jnp.where(valid, product(ahead & before) * passed, 0.0)
                enter = enter + weight[:, None, None] * got
            if dim != levels[-1]:
                term = product(ahead)[:, None, None] * got
                summed = term if summed is None else summed + term
        passed = passed * product((index > me) if reverse else (index < me))
        if dim != levels[-1]:
            crossed = total = summed
    return enter.reshape(state.shape), crossed


VMEM_ROOM = 60 * 2**20
SIDE = 128


def dims(a, b, exact=None):
    return functools.partial(
        lax.dot_general,
        dimension_numbers=(((a,), (b,)), ((), ())),
        precision=exact,
        preferred_element_type=F32,
    )


rows_cols = dims(1, 0)
rows_rows = dims(1, 1)
cols_cols = dims(0, 0)
exact_rc = dims(1, 0, PRECISE)
exact_rr = dims(1, 1, PRECISE)
exact_cc = dims(0, 0, PRECISE)


def call(body, name, shapes, flops, scratch=(), grid=None, in_specs=None, out_specs=None, moved=0):
    kw = {}
    if grid is not None:
        kw = dict(grid=grid, in_specs=in_specs, out_specs=out_specs)
    return pl.pallas_call(
        body,
        out_shape=shapes,
        scratch_shapes=list(scratch),
        name=name,
        compiler_params=pltpu.CompilerParams(vmem_limit_bytes=VMEM_ROOM),
        cost_estimate=pl.CostEstimate(flops=flops, bytes_accessed=moved, transcendentals=0),
        **kw,
    )


def half_lanes(n):
    return lax.broadcasted_iota(jnp.int32, (n, SIDE), 1) < LHD


def two_heads(values, low_half):
    none = jnp.zeros_like(values)
    return jnp.concatenate(
        [jnp.where(low_half, values, none), jnp.where(low_half, none, values)], axis=0
    )


def own_patch(n):
    row = lax.broadcasted_iota(jnp.int32, (n, n), 0)
    col = lax.broadcasted_iota(jnp.int32, (n, n), 1)
    return lax.div(row, PATCH) == lax.div(col, PATCH)


def gathered(values, mine):
    n = values.shape[0]
    kept = jnp.where(mine, values, 0.0).reshape(n // PATCH, PATCH, n)
    return jnp.sum(kept, axis=0)


def widened(values, mine):
    n = mine.shape[0]
    return jnp.where(mine, jnp.concatenate([values] * (n // PATCH), axis=0), 0.0).astype(BF)


def soft_block(scores, mine):
    n = scores.shape[0]
    key = lax.broadcasted_iota(jnp.int32, (PATCH, n), 0)
    query = lax.rem(lax.broadcasted_iota(jnp.int32, (PATCH, n), 1), PATCH)
    block = jnp.where(key <= query, gathered(scores, mine) * (LHD ** (-0.5)), -BIG)
    weights = jnp.exp(block - jnp.max(block, axis=0, keepdims=True))
    return weights / jnp.sum(weights, axis=0, keepdims=True)


def attend_body(width, qkv, out):
    n = qkv.shape[0]
    mine = own_patch(n)
    low_half = half_lanes(n)
    for p in range(width // SIDE):
        at = [slice(j * width + p * SIDE, j * width + (p + 1) * SIDE) for j in range(3)]
        q, k, v = qkv[:, at[0]], qkv[:, at[1]], qkv[:, at[2]]
        scores = rows_rows(two_heads(k, low_half), q)
        soft = [widened(soft_block(scores[j * n : (j + 1) * n], mine), mine) for j in range(2)]
        both = cols_cols(jnp.concatenate(soft, axis=0), two_heads(v, low_half))
        out[:, at[0]] = both.astype(BF)


def attend(qkv):
    rows, three = qkv.shape
    width = three // 3
    return call(
        functools.partial(attend_body, width),
        "attend",
        jax.ShapeDtypeStruct((rows, width), BF),
        rows * SIDE * width * 8,
        grid=(rows // SIDE,),
        in_specs=[pl.BlockSpec((SIDE, three), lambda i: (i, 0))],
        out_specs=pl.BlockSpec((SIDE, width), lambda i: (i, 0)),
        moved=rows * width * 8,
    )(qkv)


def attend_back_body(width, qkv, grad, out):
    n = qkv.shape[0]
    mine = own_patch(n)
    low_half = half_lanes(n)
    scale = LHD ** (-0.5)
    for p in range(width // SIDE):
        at = [slice(j * width + p * SIDE, j * width + (p + 1) * SIDE) for j in range(3)]
        q, k, v = qkv[:, at[0]], qkv[:, at[1]], qkv[:, at[2]]
        g = grad[:, at[0]]
        k_two = two_heads(k, low_half)
        scores = rows_rows(k_two, q)
        probs = rows_rows(two_heads(v, low_half), g)
        soft_wide, back_wide = [], []
        for j in range(2):
            rows = slice(j * n, (j + 1) * n)
            soft = soft_block(scores[rows], mine)
            prob = gathered(probs[rows], mine)
            back = soft * (prob - jnp.sum(soft * prob, axis=0, keepdims=True))
            soft_wide.append(widened(soft, mine))
            back_wide.append(widened(back, mine))
        q_grad = cols_cols(jnp.concatenate(back_wide, axis=0), k_two)
        k_grad = rows_cols(jnp.concatenate(back_wide, axis=1), two_heads(q, low_half))
        v_grad = rows_cols(jnp.concatenate(soft_wide, axis=1), two_heads(g, low_half))
        out[:, at[0]] = (q_grad * scale).astype(BF)
        out[:, at[1]] = (k_grad * scale).astype(BF)
        out[:, at[2]] = v_grad.astype(BF)


def attend_back(qkv, grad):
    rows, three = qkv.shape
    width = three // 3
    return call(
        functools.partial(attend_back_body, width),
        "attend_back",
        jax.ShapeDtypeStruct((rows, three), BF),
        rows * SIDE * width * 20,
        grid=(rows // SIDE,),
        in_specs=[
            pl.BlockSpec((SIDE, three), lambda i: (i, 0)),
            pl.BlockSpec((SIDE, width), lambda i: (i, 0)),
        ],
        out_specs=pl.BlockSpec((SIDE, three), lambda i: (i, 0)),
        moved=rows * width * 14,
    )(qkv, grad)


def middle_body(step, normed, grad, w_down, w_pair, hidden, pair):
    x = normed[...]
    gate = rows_cols(x, w_pair[:, :step])
    up = rows_cols(x, w_pair[:, step:])
    back = rows_cols(grad[...], w_down[...])
    sig = 1.0 / (1.0 + jnp.exp(-gate))
    act = gate * sig
    hidden[...] = (act * up).astype(BF)
    pair[:, step:] = (back * act).astype(BF)
    pair[:, :step] = (back * up * sig * (1.0 + gate * (1.0 - sig))).astype(BF)


def middle(normed, grad, w_all, ff, step):
    rows, width = normed.shape
    return call(
        functools.partial(middle_body, step),
        "middle",
        (jax.ShapeDtypeStruct((rows, ff), BF), jax.ShapeDtypeStruct((rows, 2 * ff), BF)),
        rows * width * ff * 6,
        grid=(ff // step,),
        in_specs=[
            pl.BlockSpec((rows, width), lambda i: (0, 0)),
            pl.BlockSpec((rows, width), lambda i: (0, 0)),
            pl.BlockSpec((width, step), lambda i: (0, i)),
            pl.BlockSpec((width, 2 * step), lambda i: (0, i + ff // (2 * step))),
        ],
        out_specs=(
            pl.BlockSpec((rows, step), lambda i: (0, i)),
            pl.BlockSpec((rows, 2 * step), lambda i: (0, i)),
        ),
        moved=rows * width * 4 + width * ff * 6 + rows * ff * 6,
    )(normed, grad, w_all, w_all)


def products_body(starts, *refs):
    count = len(starts) - 1
    out = refs[2 * count]
    for j in range(count):

        @pl.when((pl.program_id(0) >= starts[j]) & (pl.program_id(0) < starts[j + 1]))
        def _(j=j):
            out[...] = rows_cols(refs[2 * j][...], refs[2 * j + 1][...]).astype(out.dtype)


def products(pairs, step):
    starts = [0]
    in_specs, args, flops, moved = [], [], 0, 0
    for left, right in pairs:
        first, runs = starts[-1], right.shape[1] // step
        starts.append(first + runs)
        in_specs.append(pl.BlockSpec(left.shape, lambda i: (0, 0)))

        def column(i, first=first, runs=runs):
            return (0, jnp.clip(i - first, 0, runs - 1))

        in_specs.append(pl.BlockSpec((right.shape[0], step), column))
        args += [left, right]
        flops += 2 * left.shape[0] * right.shape[0] * right.shape[1]
        moved += 2 * (left.size + right.size)
    m = pairs[0][0].shape[0]
    return call(
        functools.partial(products_body, tuple(starts)),
        "products",
        jax.ShapeDtypeStruct((m, starts[-1] * step), BF),
        flops,
        grid=(starts[-1],),
        in_specs=in_specs,
        out_specs=pl.BlockSpec((m, step), lambda i: (0, i)),
        moved=moved + 2 * m * starts[-1] * step,
    )(*args)


def softplus_fn(values):
    return jnp.log1p(jnp.exp(-jnp.abs(values))) + jnp.maximum(values, 0.0)


def lower_ones(n):
    row = lax.broadcasted_iota(jnp.int32, (n, n), 0)
    col = lax.broadcasted_iota(jnp.int32, (n, n), 1)
    return row >= col


def taps_fill(rim, mixed, buf, taps):
    buf[0:8, :] = rim[...].astype(F32)
    buf[8 : 8 + mixed.shape[0], :] = mixed[...].astype(F32)


def conv_here(buf, k_x, k_bc, info, n, taps):
    wide = jnp.concatenate([k_x[...], k_bc[...]], axis=1)
    total = None
    for k in range(taps):
        at = 9 - taps + k
        term = buf[at : at + n, :] * wide[k : k + 1, :] * info[:, k : k + 1]
        total = term if total is None else total + term
    return total


def decays(raw, small, n):
    base = raw[...] + small[0:1, :]
    step = softplus_fn(base)
    rate = jnp.exp(small[1:2, :])
    log_decay = -step * rate
    tri = lower_ones(n).astype(F32)
    cum = exact_rc(tri, log_decay)
    return base, step, rate, log_decay, tri, cum


def mix_body(taps, inner, rim, mixed, raw, small, skip, k_x, k_bc, info, seg, y_out, c_out, din_out, state_out, buf):
    n = mixed.shape[0]
    taps_fill(rim, mixed, buf, taps)
    pre = conv_here(buf, k_x, k_bc, info, n, taps)
    act = pre / (1.0 + jnp.exp(-pre))
    b = act[:, inner : inner + SIDE]
    c = act[:, inner + SIDE :]
    _, step, _, _, _, cum = decays(raw, small, n)
    cum_t, step_t = cum.T, step.T
    live = lower_ones(n) & (info[:, 6:7] == seg[0:1, :])
    both = exact_rr(c, b)
    din_out[...] = info[:, 4:5] * jnp.exp(cum)
    tail = jnp.exp(jnp.where(info[:, 5:6] > 0.0, cum[n - 1 : n, :] - cum, -BIG)) * step
    low_half = half_lanes(n)
    c_out[...] = c
    for p in range(inner // SIDE):
        at = slice(p * SIDE, (p + 1) * SIDE)
        x = act[:, at]
        y = skip[0:1, at] * x
        for j, mine in enumerate((low_half, ~low_half)):
            h = 2 * p + j
            gaps = jnp.exp(jnp.where(live, cum[:, h : h + 1] - cum_t[h : h + 1, :], -BIG))
            mix = both * gaps * step_t[h : h + 1, :]
            y = y + exact_rc(mix, jnp.where(mine, x, 0.0))
        y_out[:, at] = y
        weighted = x * jnp.where(low_half, tail[:, 2 * p : 2 * p + 1], tail[:, 2 * p + 1 : 2 * p + 2])
        state_out[at, :] = exact_cc(weighted, b)


def mix(rim, mixed, raw, small, skip, k_x, k_bc, info, seg):
    n, wide = mixed.shape
    taps, inner = k_x.shape
    return call(
        functools.partial(mix_body, taps, inner),
        "mix",
        (
            jax.ShapeDtypeStruct((n, inner), F32),
            jax.ShapeDtypeStruct((n, SIDE), F32),
            jax.ShapeDtypeStruct((n, SIDE), F32),
            jax.ShapeDtypeStruct((inner, SIDE), F32),
        ),
        n * n * inner * 24,
        scratch=(pltpu.VMEM((n + 8, wide), F32),),
        moved=n * inner * 20,
    )(rim, mixed, raw, small, skip, k_x, k_bc, info, seg)


def pair_cols(values, p, low_half):
    return jnp.where(low_half, values[:, 2 * p : 2 * p + 1], values[:, 2 * p + 1 : 2 * p + 2])


def finish_body(inner, y_part, c, din, state, z, y_out, gated_out, square):
    n = y_part.shape[0]
    low_half = half_lanes(n)
    total = None
    for p in range(inner // SIDE):
        at = slice(p * SIDE, (p + 1) * SIDE)
        y = y_part[:, at] + pair_cols(din, p, low_half) * exact_rr(c[...], state[at, :])
        gate = z[:, at]
        gated = y * (gate / (1.0 + jnp.exp(-gate)))
        y_out[:, at] = y
        gated_out[:, at] = gated
        term = gated * gated
        total = term if total is None else total + term
    square[...] = jnp.broadcast_to(jnp.sum(total, axis=1, keepdims=True), square.shape)


def finish(y_part, c, din, state, z):
    n, inner = y_part.shape
    return call(
        functools.partial(finish_body, inner),
        "finish",
        (
            jax.ShapeDtypeStruct((n, inner), F32),
            jax.ShapeDtypeStruct((n, inner), F32),
            jax.ShapeDtypeStruct((n, SIDE), F32),
        ),
        n * SIDE * inner * 12,
        moved=n * inner * 20,
    )(y_part, c, din, state, z)


def unfinish_body(inner, y_norm_grad, gated, y_full, z, gain, stats, din, c, y_grad, z_grad, state_grad):
    n = gated.shape[0]
    low_half = half_lanes(n)
    for p in range(inner // SIDE):
        at = slice(p * SIDE, (p + 1) * SIDE)
        back = stats[:, 0:1] * (y_norm_grad[:, at] * gain[0:1, at]) - gated[:, at] * stats[:, 1:2]
        gate = z[:, at]
        sig = 1.0 / (1.0 + jnp.exp(-gate))
        y_back = back * gate * sig
        y_grad[:, at] = y_back
        z_grad[:, at] = (back * y_full[:, at] * sig * (1.0 + gate * (1.0 - sig))).astype(BF)
        state_grad[at, :] = exact_cc(y_back * pair_cols(din, p, low_half), c[...])


def unfinish(y_norm_grad, gated, y_full, z, gain, stats, din, c):
    n, inner = gated.shape
    return call(
        functools.partial(unfinish_body, inner),
        "unfinish",
        (
            jax.ShapeDtypeStruct((n, inner), F32),
            jax.ShapeDtypeStruct((n, inner), BF),
            jax.ShapeDtypeStruct((inner, SIDE), F32),
        ),
        n * SIDE * inner * 12,
        moved=n * inner * 24,
    )(y_norm_grad, gated, y_full, z, gain, stats, din, c)


def unmix_body(
    taps, inner, rim, mixed, raw, small, skip, k_x, k_bc, info, seg, y_grad, state_in, state_back,
    ext_out, raw_out, taps_out, heads_out, skip_out, buf, d_buf, d_act, cols, sums, steps,
):
    n = mixed.shape[0]
    taps_fill(rim, mixed, buf, taps)
    pre = conv_here(buf, k_x, k_bc, info, n, taps)
    sig_pre = 1.0 / (1.0 + jnp.exp(-pre))
    act = pre * sig_pre
    b = act[:, inner : inner + SIDE]
    c = act[:, inner + SIDE :]
    base, step, rate, log_decay, tri, cum = decays(raw, small, n)
    cum_t, step_t = cum.T, step.T
    live = lower_ones(n) & (info[:, 6:7] == seg[0:1, :])
    both = exact_rr(c, b)
    din = info[:, 4:5] * jnp.exp(cum)
    tail = jnp.exp(jnp.where(info[:, 5:6] > 0.0, cum[n - 1 : n, :] - cum, -BIG))
    low_half = half_lanes(n)
    cols[...] = jnp.zeros_like(cols)
    sums[...] = jnp.zeros_like(sums)
    steps[...] = jnp.zeros_like(steps)
    both_grad = jnp.zeros((n, n), F32)
    b_grad = jnp.zeros((n, SIDE), F32)
    c_grad = jnp.zeros((n, SIDE), F32)
    lane = lax.broadcasted_iota(jnp.int32, (1, SIDE), 1)
    total_grad = jnp.zeros((1, SIDE), F32)
    tail_grad = jnp.zeros((n, SIDE), F32)
    for p in range(inner // SIDE):
        at = slice(p * SIDE, (p + 1) * SIDE)
        x = act[:, at]
        dy = y_grad[:, at]
        s_in = state_in[at, :]
        s_back = state_back[at, :]
        out_b = exact_rr(b, s_back)
        weight = pair_cols(tail, p, low_half) * pair_cols(step, p, low_half)
        dx = skip[0:1, at] * dy + weight * out_b
        b_grad = b_grad + exact_rc(x * weight, s_back)
        dy_in = pair_cols(din, p, low_half) * dy
        in_c = exact_rr(c, s_in)
        c_grad = c_grad + exact_rc(dy_in, s_in)
        skip_out[0:1, at] = jnp.sum(dy * x, axis=0, keepdims=True)
        held = jnp.sum(s_in * s_back, axis=1, keepdims=True)
        for j, mine in enumerate((low_half, ~low_half)):
            h = 2 * p + j
            dy_mine = jnp.where(mine, dy, 0.0)
            gaps = jnp.exp(jnp.where(live, cum[:, h : h + 1] - cum_t[h : h + 1, :], -BIG))
            step_row = step_t[h : h + 1, :]
            back = exact_rr(dy_mine, x) * gaps
            both_grad = both_grad + back * step_row
            back = back * both
            each = back * step_row
            dx = dx + exact_cc(both * gaps * step_row, dy_mine)
            steps[h : h + 1, :] = jnp.sum(back, axis=0, keepdims=True)
            sums[h : h + 1, :] = -jnp.sum(each, axis=0, keepdims=True)
            from_in = jnp.sum(jnp.where(mine, dy_in * in_c, 0.0), axis=1, keepdims=True)
            cols[:, h : h + 1] = jnp.sum(each, axis=1, keepdims=True) + from_in
            from_tail = jnp.sum(jnp.where(mine, x * out_b, 0.0), axis=1, keepdims=True)
            tail_grad = tail_grad + jnp.where(lane == h, from_tail, 0.0)
            here = jnp.sum(held[j * LHD : (j + 1) * LHD, :], axis=0, keepdims=True)
            total_grad = total_grad + jnp.where(lane == h, here, 0.0)
        d_act[:, at] = dx
    d_act[:, inner : inner + SIDE] = b_grad + exact_cc(both_grad, c)
    d_act[:, inner + SIDE :] = c_grad + exact_rc(both_grad, b)
    tail_back = tail_grad * tail
    row = lax.broadcasted_iota(jnp.int32, (n, SIDE), 0)
    moved = tail_back * step
    last = jnp.sum(moved, axis=0, keepdims=True) + total_grad * din[n - 1 : n, :]
    cum_grad = cols[...] + sums[...].T - moved + jnp.where(row == n - 1, last, 0.0)
    decay_grad = exact_cc(tri, cum_grad)
    step_grad = steps[...].T + tail_back - decay_grad * rate
    raw_grad = step_grad / (1.0 + jnp.exp(-base))
    raw_out[...] = raw_grad
    heads_out[0:1, :] = jnp.sum(raw_grad, axis=0, keepdims=True)
    heads_out[1:2, :] = jnp.sum(decay_grad * log_decay, axis=0, keepdims=True)
    heads_out[2:8, :] = jnp.zeros((6, SIDE), F32)
    d_pre = d_act[...] * (sig_pre * (1.0 + pre * (1.0 - sig_pre)))
    d_buf[...] = jnp.zeros_like(d_buf)
    wide = jnp.concatenate([k_x[...], k_bc[...]], axis=1)
    for k in range(taps):
        at = 9 - taps + k
        masked = d_pre * info[:, k : k + 1]
        d_buf[at : at + n, :] = d_buf[at : at + n, :] + masked * wide[k : k + 1, :]
        taps_out[k : k + 1, :] = jnp.sum(masked * buf[at : at + n, :], axis=0, keepdims=True)
    ext_out[...] = d_buf[...]


def unmix(rim, mixed, raw, small, skip, k_x, k_bc, info, seg, y_grad, state_in, state_back):
    n, wide = mixed.shape
    taps, inner = k_x.shape
    return call(
        functools.partial(unmix_body, taps, inner),
        "unmix",
        (
            jax.ShapeDtypeStruct((n + 8, wide), F32),
            jax.ShapeDtypeStruct((n, SIDE), F32),
            jax.ShapeDtypeStruct((taps, wide), F32),
            jax.ShapeDtypeStruct((8, SIDE), F32),
            jax.ShapeDtypeStruct((1, inner), F32),
        ),
        n * n * inner * 96,
        scratch=(
            pltpu.VMEM((n + 8, wide), F32),
            pltpu.VMEM((n + 8, wide), F32),
            pltpu.VMEM((n, wide), F32),
            pltpu.VMEM((n, SIDE), F32),
            pltpu.VMEM((SIDE, n), F32),
            pltpu.VMEM((SIDE, n), F32),
        ),
        moved=n * inner * 30,
    )(rim, mixed, raw, small, skip, k_x, k_bc, info, seg, y_grad, state_in, state_back)


def bf_dot(left, right):
    return rows_cols(left, right)


def dot_t(left, right):
    return rows_rows(left, right)


def grad_dot(left, right):
    return cols_cols(left, right)


def rms_rows(values):
    return lax.rsqrt(jnp.mean(values * values, axis=-1, keepdims=True) + EPS)


def norm_back(grad_in, values, rstd_rows, gain_row):
    normed_rows = values * rstd_rows
    gain_grad = jnp.sum(grad_in * normed_rows, axis=0)
    scaled = grad_in * gain_row[None, :]
    input_grad = rstd_rows * (
        scaled - normed_rows * jnp.mean(scaled * normed_rows, axis=-1, keepdims=True)
    )
    return (input_grad, gain_grad)


def local(
    seq_count,
    bytes_in,
    out_grad,
    seq_ids,
    norm_gain,
    w_z,
    w_x,
    w_bc,
    w_dt,
    w_out,
    attn_gain,
    w_q,
    w_k,
    w_v,
    w_o,
    mlp_gain,
    w_gate,
    w_up,
    w_down,
    dt_bias,
    a_log,
    d_skip,
    conv_x,
    conv_bc,
    inner_gain,
):
    grid = Grid(seq_count)
    rows, ff = w_gate.shape
    inner = w_x.shape[1]
    bc_width = w_bc.shape[1]
    heads = w_dt.shape[1]
    attn_width = w_q.shape[1]
    step = min(256, ff)
    byte_rows, model_width = bytes_in.shape
    patch_rows = byte_rows // PATCH
    taps = conv_x.shape[0]
    inner_full = inner * lax.axis_size("mp")

    first = jnp.concatenate(
        [
            w_x.astype(BF),
            w_bc.astype(BF),
            w_dt.astype(BF),
            norm_gain.astype(BF)[:, None],
            attn_gain.astype(BF)[:, None],
            mlp_gain.astype(BF)[:, None],
            jnp.zeros((rows, SIDE - heads - 3), BF),
        ],
        axis=1,
    )
    first_column = gather_column(grid, first)
    first_all = gather_plane(grid, first_column)
    second = jnp.concatenate(
        [w.astype(BF) for w in (w_z, w_out.T, w_q, w_k, w_v, w_o.T)], axis=1
    )
    second = follow(second, first_column)
    pair = jnp.stack(
        [w.astype(BF).reshape(rows, ff // step, step) for w in (w_gate, w_up)], axis=2
    ).reshape(rows, 2 * ff)
    mlp = jnp.concatenate([w_down.T.astype(BF), pair], axis=1)

    tail_all = first_all[:, inner + bc_width :]
    gains = tail_all[:, heads : heads + 3].astype(F32).T
    norm_row, attn_row, mlp_row = gains[0], gains[1], gains[2]
    x_float = bytes_in.astype(F32)
    patch_in = jnp.mean(x_float.reshape(patch_rows, PATCH, model_width), axis=1)
    rstd_patch = rms_rows(patch_in)
    h_norm = (patch_in * rstd_patch * norm_row[None, :]).astype(BF)
    into = bf_dot(h_norm, first_all)
    mixed = into[:, : inner + bc_width].astype(BF)
    raw = into[:, inner + bc_width :]
    second_column = gather_column(grid, second, mixed)
    second_all = gather_plane_off(grid, second_column).reshape(model_width, -1)
    z_all, out_all = second_all[:, :inner], second_all[:, inner : 2 * inner]
    third_all = second_all[:, 2 * inner :]
    qkv_all, wo_all = third_all[:, : 3 * attn_width], third_all[:, 3 * attn_width :]
    rim = lax.ppermute(
        mixed[patch_rows - (taps - 1) :], "seq", [(i, i + 1) for i in range(seq_count - 1)]
    )
    rim = jnp.pad(rim, ((8 - (taps - 1), 0), (0, 0)))
    first_row = lax.axis_index("seq") * patch_rows
    ids_padded = jnp.concatenate([jnp.full((taps - 1,), -1, jnp.int32), seq_ids])
    ids_ext = lax.dynamic_slice_in_dim(ids_padded, first_row, patch_rows + taps - 1)
    ids = ids_ext[taps - 1 :]
    columns = [ids_ext[k : k + patch_rows] == ids for k in range(taps)]
    columns += [ids == ids_ext[taps - 2], ids == ids[patch_rows - 1], ids]
    info = jnp.stack([c.astype(F32) for c in columns], axis=1)
    info = jnp.pad(info, ((0, 0), (0, SIDE - info.shape[1])))
    seg = jnp.broadcast_to(ids.astype(F32)[None, :], (8, patch_rows))
    small = jnp.pad(jnp.stack([dt_bias, a_log]), ((0, 6), (0, SIDE - heads)))
    skip = jnp.repeat(d_skip, inner // heads)[None, :]
    whole = jnp.sum(softplus_fn(raw[:, :heads] + dt_bias), axis=0) * -jnp.exp(a_log)
    table = spread_small(grid, info[patch_rows - 1, taps] * jnp.exp(whole))
    known = (rim, mixed, raw, small, skip, conv_x, conv_bc, info, seg)
    y_part, c_rows, decay_in, state_own = mix(*known)
    state_in, (crossed, _) = scan_states(grid, table, state_own, False)
    mlp_column = gather_column(grid, follow(mlp, first_all, second_column), crossed)
    mlp_all = gather_plane_off(grid, follow(mlp_column, second_all)).reshape(model_width, -1)
    down_all, pair_all = mlp_all[:, :ff], mlp_all[:, ff:]
    gate_z = bf_dot(h_norm, z_all)
    y_full, gated, square = finish(y_part, c_rows, decay_in, state_in, gate_z)
    square_sum = mp_sum_exact(square[:, 0])
    rstd_inner = lax.rsqrt(square_sum / inner_full + EPS)[:, None]
    y_norm = (gated * rstd_inner * inner_gain[None, :]).astype(BF)
    mixer_out = mp_sum(dot_t(y_norm, out_all))
    patch_out = patch_in + mixer_out

    rows_in = x_float + jnp.repeat(patch_out, PATCH, axis=0)
    rstd_attn = rms_rows(rows_in)
    normed = (rows_in * rstd_attn * attn_row[None, :]).astype(BF)
    qkv = bf_dot(normed, qkv_all).astype(BF)
    attended = attend(qkv)
    after_attn = rows_in + mp_sum(dot_t(attended, wo_all))
    rstd_mlp = rms_rows(after_attn)
    normed_mlp = (after_attn * rstd_mlp * mlp_row[None, :]).astype(BF)
    hidden, pair_grad = middle(normed_mlp, out_grad, mlp_all, ff, step)
    block_out = after_attn + mp_sum(dot_t(hidden, down_all))

    mlp_part = products(
        (
            (plane_major(grid, normed_mlp), pair_grad),
            (plane_major(grid, out_grad), hidden),
        ),
        4 * step,
    )
    mlp_plane = scatter_plane(grid, mlp_part)
    pair_grad = follow(pair_grad, mlp_part)
    mlp_norm_grad = mp_sum(dot_t(pair_grad, pair_all))
    mlp_in_grad, mlp_gain_grad = norm_back(mlp_norm_grad, after_attn, rstd_mlp, mlp_row)
    after_grad = out_grad.astype(F32) + mlp_in_grad
    after_low = after_grad.astype(BF)
    attended_grad = bf_dot(after_low, wo_all).astype(BF)
    qkv_grad = attend_back(qkv, attended_grad)
    attn_norm_grad = mp_sum(dot_t(qkv_grad, qkv_all))
    attn_in_grad, attn_gain_grad = norm_back(attn_norm_grad, rows_in, rstd_attn, attn_row)
    rows_grad = after_grad + attn_in_grad
    patch_grad = jnp.sum(rows_grad.reshape(patch_rows, PATCH, model_width), axis=1)
    patch_low = patch_grad.astype(BF)
    y_norm_grad = bf_dot(patch_low, out_all)
    shared = y_norm_grad * gated
    inner_gain_grad = jnp.sum(shared * rstd_inner, axis=0)
    cross_sum = mp_sum_exact(jnp.sum(shared * inner_gain[None, :], axis=-1))[:, None]
    stats = jnp.concatenate([rstd_inner, rstd_inner**3 * (cross_sum / inner_full)], axis=1)
    stats = jnp.pad(stats, ((0, 0), (0, SIDE - 2)))
    y_grad, z_low, state_in_grad = unfinish(
        y_norm_grad, gated, y_full, gate_z, inner_gain[None, :], stats, decay_in, c_rows
    )
    h_norm_t = plane_major(grid, h_norm)
    rest_part = products(
        (
            (plane_major(grid, normed), qkv_grad),
            (plane_major(grid, after_low), attended),
            (h_norm_t, z_low),
            (plane_major(grid, patch_low), y_norm),
        ),
        attn_width,
    )
    state_in_grad = follow(state_in_grad, rest_part)
    state_grad, (crossed, sent) = scan_states(grid, table, state_in_grad, True, mlp_plane)
    rest_plane = scatter_plane(grid, follow(rest_part, mlp_plane, crossed))
    mlp_sums = [
        scatter_column(grid, follow(mlp_plane[:, i : i + ff], sent)) for i in (0, ff, 2 * ff)
    ]
    ext_grad, raw_grad, taps_grad, heads_grad, skip_grad = unmix(
        *known, y_grad, state_in, state_grad
    )
    bc_total = mp_sum(ext_grad[:, inner:])
    conv_bc_grad = mp_sum_exact(taps_grad[:, inner:])
    ext_full = jnp.concatenate([ext_grad[:, :inner], bc_total], axis=1)
    rim_back = lax.ppermute(
        ext_full[8 - (taps - 1) : 8], "seq", [(i + 1, i) for i in range(seq_count - 1)]
    )
    mixed_low = (
        ext_full[8:] + jnp.pad(rim_back, ((patch_rows - (taps - 1), 0), (0, 0)))
    ).astype(BF)
    first_grad = jnp.concatenate([mixed_low, raw_grad.astype(BF)], axis=1)
    first_grad = follow(first_grad, mlp_sums[0])
    first_part = bf_dot(h_norm_t, first_grad).astype(BF)
    first_grad = follow(first_grad, first_part)
    first_plane = scatter_plane(grid, follow(first_part, rest_plane))
    lane = lax.broadcasted_iota(jnp.int32, (1, first_grad.shape[1]), 1)
    twice = (lane >= inner) & (lane < inner + bc_width) & (lax.axis_index("mp") > 0)
    cut = 4 * attn_width
    rest_sums = [
        scatter_column(grid, part) for part in (rest_plane[:, :cut], rest_plane[:, cut:])
    ]
    first_grad = follow(first_grad, mlp_sums[1])
    own_grad = jnp.where(twice, jnp.zeros_like(first_grad), first_grad)
    h_grad = mp_sum(dot_t(own_grad, first_all) + dot_t(z_low, z_all))
    patch_in_grad, norm_gain_grad = norm_back(h_grad, patch_in, rstd_patch, norm_row)
    patch_total = follow(patch_grad + patch_in_grad, rest_sums[1])
    bytes_grad = rows_grad + jnp.repeat(patch_total / PATCH, PATCH, axis=0)

    pair_sum = jnp.concatenate(mlp_sums[:2], axis=1).reshape(rows, ff // step, 2, step)
    w_gate_grad = pair_sum[:, :, 0].reshape(rows, ff)
    w_up_grad = pair_sum[:, :, 1].reshape(rows, ff)
    w_down_grad = mlp_sums[2].T
    first_sum = scatter_column(grid, first_plane)
    w_qkv_grad, w_o_grad = (
        rest_sums[0][:, : 3 * attn_width],
        rest_sums[0][:, 3 * attn_width :].T,
    )
    w_z_grad, w_out_grad = rest_sums[1][:, :inner], rest_sums[1][:, inner:].T

    pieces = (
        heads_grad[:2],
        skip_grad,
        taps_grad[:, :inner],
        conv_bc_grad,
        inner_gain_grad,
        norm_gain_grad,
        attn_gain_grad,
        mlp_gain_grad,
    )
    flat = seq_sum(jnp.concatenate([p.reshape(-1, SIDE) for p in pieces], axis=0))
    parts, start = [], 0
    for p in pieces:
        stop = start + p.size // SIDE
        parts.append(flat[start:stop].reshape(p.shape))
        start = stop
    mine = lax.axis_index("seq") * rows
    gain_parts = [lax.dynamic_slice_in_dim(g, mine, rows) for g in parts[5:]]
    return (
        block_out,
        bytes_grad,
        gain_parts[0],
        w_z_grad,
        first_sum[:, :inner],
        first_sum[:, inner : inner + bc_width],
        first_sum[:, inner + bc_width : inner + bc_width + heads],
        w_out_grad,
        gain_parts[1],
        w_qkv_grad[:, :attn_width],
        w_qkv_grad[:, attn_width : 2 * attn_width],
        w_qkv_grad[:, 2 * attn_width :],
        w_o_grad,
        gain_parts[2],
        w_gate_grad,
        w_up_grad,
        w_down_grad,
        parts[0][0, :heads],
        parts[0][1, :heads],
        jnp.sum(parts[1].reshape(heads, inner // heads), axis=1),
        parts[2],
        parts[3],
        parts[4],
    )


def solution(mesh):
    rows, cols, both, rest = P("seq", None), P("seq", "mp"), P("mp", "seq"), P()
    vec, per = P("seq"), P("mp")
    weights = (vec, cols, cols, rows, cols, both, vec, cols, cols, cols, both, vec, cols, cols, both)
    small = (per, per, per, P(None, "mp"), rest, per)
    in_specs = (rows, rows, rest) + weights + small
    out_specs = (rows, rows) + weights + small
    body = functools.partial(local, mesh.shape["seq"])
    return jax.shard_map(body, mesh=mesh, in_specs=in_specs, out_specs=out_specs, check_vma=False)
```
